32 devices in a mesh: dp: 4 (over y, x), expert: 8 (over z, core).
Axes of the slice: x: 2, y: 2, z: 4, core: 2. Of those that a mesh axis runs over, the one named last changes fastest.
Arguments:
- tokens: bfloat16 [4096, 1024], P(('dp', 'expert')), may hold values from -6 to 6
- routes: int32 [4096, 8], P(('dp', 'expert')), may hold values from 0 to 15, all different within a row; in each aligned block of 128 rows (0 to 127, 128 to 255, ...) at most 80 rows name the same one
- route_weights: float32 [4096, 8], P(('dp', 'expert')), may hold values from 0.03 to 0.5
- gate_weight: bfloat16 [16, 1024, 512], P('expert'), may hold values from -0.1875 to 0.1875
- up_weight: bfloat16 [16, 1024, 512], P('expert'), may hold values from -0.1875 to 0.1875
- down_weight: bfloat16 [16, 512, 1024], P('expert'), may hold values from -0.25 to 0.25
- cotangent: bfloat16 [4096, 1024], P(('dp', 'expert')), may hold values from -6 to 6
Outputs:
- layer_out: bfloat16 [4096, 1024], P(('dp', 'expert'))
- token_grads: bfloat16 [4096, 1024], P(('dp', 'expert'))
- route_grads: float32 [4096, 8], P(('dp', 'expert'))
- gate_grads: float32 [16, 1024, 512], P('expert', 'dp')
- up_grads: float32 [16, 1024, 512], P('expert', 'dp')
- down_grads: float32 [16, 512, 1024], P('expert', 'dp')
The draws below stay inside these ranges and needn't reach their ends.
Inputs may be any that keep to these rules, and one draw needn't show every extreme that they name: `routes`: A token names 8 different experts. Among the token-route pairs of one device's 128 tokens (aligned blocks of rows), no expert is named more than 80 times, a bound that some block reaches.
All inputs are finite; a program needn't handle non-finite values.
Results may differ from the reference program's by a relative error of at most 0.0065.
Values may be sent and summed in bfloat16 or wider, within the bound.
No kernel may reach another device: no remote copies, remote signals or barrier semaphores. Data moves between devices by JAX's collectives and lax.ppermute only.
A program may use at most 128 MiB of HBM per device.

```python
import math
import jax
import jax.numpy as jnp
import numpy as np
from jax import lax

D = 1024
FF = 512
TOP = 8
TOK_DEV = 128
EXPERTS = 16
TOKENS = 4096
CAP = 80


def steps_of(stream_key, extent, shards, low, high):
    level = 1.0
    for dim, parts in shards:
        draws = jax.random.uniform(jax.random.fold_in(jax.random.fold_in(stream_key, 6), dim), (parts,), jnp.float32, low / len(shards), high / len(shards))
        level = level * jnp.repeat(jnp.exp(draws), extent[dim] // parts).reshape((-1,) + (1,) * (len(extent) - 1 - dim))
    return level


def deal_out(key, own, number, rows, count, top, most, skew):
    ranking = jax.random.permutation(key, count)
    heavy_load, common = load_shares(count, rows * top, most, skew, True), load_shares(count, rows * top, most, skew, False)
    places = jnp.arange(count)

    def named(lengths, rotation):
        used = int((lengths > 0).sum())
        fixed = max(1, used // 4)
        moved = fixed + (places - fixed + rotation * (used - fixed)) % max(1, count - fixed)
        return jnp.zeros((count,), jnp.int32).at[ranking[jnp.where(places < fixed, places, moved)]].set(jnp.asarray(lengths, jnp.int32))

    lengths = jnp.where(number % 4 == 0, named(heavy_load, number // 4), named(common, number - number // 4 - 1))
    mixed = jax.random.permutation(jax.random.fold_in(own, 3), count)
    donor, taker = mixed[0:count // 2 * 2:2], mixed[1:count // 2 * 2:2]
    margin = jnp.minimum(lengths[donor] - 1, most - lengths[taker]) // 2
    margin = jnp.where((donor == ranking[0]) | (taker == ranking[0]) | (lengths[taker] == 0), 0, jnp.maximum(margin, 0))
    moved = jax.random.randint(jax.random.fold_in(own, 4), (count // 2,), 0, 1 << 20) % (margin + 1)
    lengths = lengths.at[donor].add(-moved).at[taker].add(moved)
    labels = jnp.searchsorted(jnp.cumsum(lengths), jnp.arange(rows * top), side="right").astype(jnp.int32)
    listing = labels.reshape(top, rows).T
    listing = listing[jax.random.permutation(jax.random.fold_in(own, 1), rows)]
    rotation = jax.random.randint(jax.random.fold_in(own, 2), (rows, 1), 0, top)
    return jnp.take_along_axis(listing, (jnp.arange(top)[None, :] + rotation) % top, axis=1)


def load_shares(count, total, bound, slope, full):
    loads = [(1 << 20) // math.isqrt(grade ** slope) + 1 for grade in range(1, count + 1)]
    largest = bound if full else min(bound, max(-(-total // count), total * loads[0] // sum(loads)))
    least = 1 if total - largest >= count - 1 else 0
    given, surplus = [largest] + [least] * (count - 1), total - largest - least * (count - 1)
    while surplus > 0:
        free = [i for i in range(1, count) if given[i] < largest] or [i for i in range(1, count) if given[i] < bound]
        mass, left = sum([loads[i] for i in free]), surplus
        for i in free:
            extra = min(bound - given[i], max(1, left * loads[i] // mass), surplus)
            given[i] = given[i] + extra
            surplus = surplus - extra
    return np.array(given)


def normal_values(stream_key, dims, spread, reach, shards=(), kind=jnp.bfloat16):
    drawn = jax.random.normal(stream_key, dims, jnp.float32) * spread
    if len(shards) > 0:
        drawn = steps_of(stream_key, dims, shards, -0.22, 0.18) * drawn
    return jnp.clip(drawn, min=-reach, max=reach).astype(kind)


def setup_inputs(seed: int = 0) -> dict:
    splits = jax.random.split(jax.random.key(seed), 8)
    tokens = normal_values(splits[0], (TOKENS, D), 1.0, 6.0, ((0, 32),))
    routes_keys = jax.random.split(jax.random.fold_in(splits[1], 1), TOKENS // TOK_DEV)
    routes_turns = jax.random.permutation(jax.random.fold_in(splits[1], 3), TOKENS // TOK_DEV)
    routes = jax.vmap(lambda own, number: deal_out(jax.random.fold_in(splits[1], 2), own, number, TOK_DEV, EXPERTS, TOP, CAP, 2))(routes_keys, routes_turns).reshape((TOKENS, TOP))
    route_weights = jnp.clip(jnp.exp(math.log(0.5) - 2.8134107 * jax.random.uniform(splits[2], (TOKENS, TOP), jnp.float32) ** steps_of(splits[2], (TOKENS, TOP), ((0, 32),), -0.2, 0.2)), 0.03, 0.5)
    gate_weight = normal_values(splits[3], (EXPERTS, D, FF), D ** -0.5, 0.1875, ((0, 8),))
    up_weight = normal_values(splits[4], (EXPERTS, D, FF), D ** -0.5, 0.1875, ((0, 8),))
    down_weight = normal_values(splits[5], (EXPERTS, FF, D), FF ** -0.5, 0.25, ((0, 8),))
    cotangent = normal_values(splits[6], (TOKENS, D), 1.0, 6.0, ((0, 32),))
    return dict(tokens=tokens, routes=routes, route_weights=route_weights, gate_weight=gate_weight, up_weight=up_weight, down_weight=down_weight, cotangent=cotangent)


def swish(values):
    return values * jax.nn.sigmoid(values)


def slot_tables(block_routes, expert_total, capacity):
    token_count = block_routes.shape[0]
    route_count = block_routes.shape[1]
    pair_total = token_count * route_count
    chosen = block_routes.reshape(pair_total)
    onehot = (chosen[:, None] == jnp.arange(expert_total, dtype=jnp.int32)[None, :]).astype(jnp.int32)
    before = jnp.cumsum(onehot, axis=0) - onehot
    position = jnp.sum(before * onehot, axis=1)
    target = chosen * capacity + position
    filler = jnp.full((expert_total * capacity,), -1, jnp.int32).at[target].set(jnp.arange(pair_total, dtype=jnp.int32))
    return target, filler


def block_filler(block_routes):
    return slot_tables(block_routes, EXPERTS, CAP)[1]


def reference(tokens, routes, route_weights, gate_weight, up_weight, down_weight, cotangent):
    blocks = TOKENS // TOK_DEV
    pair_total = TOK_DEV * TOP
    fillers = jax.vmap(block_filler)(routes.reshape(blocks, TOK_DEV, TOP))
    offsets = (jnp.arange(blocks, dtype=jnp.int32) * pair_total)[:, None]
    pair_lists = jnp.where(fillers >= 0, fillers + offsets, -1)
    pair_lists = pair_lists.reshape(blocks, EXPERTS, CAP).transpose(1, 0, 2).reshape(EXPERTS, blocks * CAP)
    flat_weights = route_weights.reshape(TOKENS * TOP)

    def expert_step(totals, inputs):
        out_acc, grad_acc, route_acc = totals
        pair_index, gate_mat, up_mat, down_mat = inputs
        occupied = pair_index >= 0
        safe_pair = jnp.maximum(pair_index, 0)
        token_index = safe_pair // TOP
        token_rows = jnp.where(occupied[:, None], tokens[token_index], jnp.zeros((), jnp.bfloat16))
        weight_col = jnp.where(occupied, flat_weights[safe_pair], jnp.float32(0.0))
        cot_rows = cotangent[token_index].astype(jnp.float32)
        gate_pre = jnp.dot(token_rows, gate_mat, preferred_element_type=jnp.float32)
        up_pre = jnp.dot(token_rows, up_mat, preferred_element_type=jnp.float32)
        sigmoid_gate = jax.nn.sigmoid(gate_pre)
        silu_gate = gate_pre * sigmoid_gate
        hidden = (silu_gate * up_pre).astype(jnp.bfloat16)
        expert_out = jnp.dot(hidden, down_mat, preferred_element_type=jnp.float32).astype(jnp.bfloat16)
        out_wide = expert_out.astype(jnp.float32)
        route_vals = jnp.where(occupied, jnp.sum(out_wide * cot_rows, axis=1), jnp.float32(0.0))
        out_grad = (weight_col[:, None] * cot_rows).astype(jnp.bfloat16)
        hidden_grad = jnp.dot(out_grad, down_mat.T, preferred_element_type=jnp.float32)
        gate_grad = (hidden_grad * up_pre * sigmoid_gate * (1.0 + gate_pre * (1.0 - sigmoid_gate))).astype(jnp.bfloat16)
        up_grad = (hidden_grad * silu_gate).astype(jnp.bfloat16)
        pair_grad = (jnp.dot(gate_grad, gate_mat.T, preferred_element_type=jnp.float32)
                     + jnp.dot(up_grad, up_mat.T, preferred_element_type=jnp.float32)).astype(jnp.bfloat16)
        out_acc = out_acc.at[token_index].add(weight_col[:, None] * out_wide)
        grad_acc = grad_acc.at[token_index].add(pair_grad.astype(jnp.float32))
        route_acc = route_acc.at[safe_pair].add(route_vals)
        gate_sum = jnp.dot(token_rows.T, gate_grad, preferred_element_type=jnp.float32)
        up_sum = jnp.dot(token_rows.T, up_grad, preferred_element_type=jnp.float32)
        down_sum = jnp.dot(hidden.T, out_grad, preferred_element_type=jnp.float32)
        return (out_acc, grad_acc, route_acc), (gate_sum, up_sum, down_sum)

    start = (jnp.zeros((TOKENS, D), jnp.float32), jnp.zeros((TOKENS, D), jnp.float32), jnp.zeros((TOKENS * TOP,), jnp.float32))
    totals, stacked = lax.scan(expert_step, start, (pair_lists, gate_weight, up_weight, down_weight))
    out_acc, grad_acc, route_acc = totals
    gate_grads, up_grads, down_grads = stacked
    return (out_acc.astype(jnp.bfloat16), grad_acc.astype(jnp.bfloat16), route_acc.reshape(TOKENS, TOP), gate_grads, up_grads, down_grads)
```

```python
import math

import jax
import jax.numpy as jnp
from jax import lax
from jax.sharding import PartitionSpec as P

BF = jnp.bfloat16
F32 = jnp.float32


def pick(v, i, axis=0):
    return lax.dynamic_index_in_dim(v, i, axis, keepdims=False)


def local(tokens, routes, route_weights, gate_weight, up_weight, down_weight, cotangent):
    dp = lax.axis_size("dp")
    ne = lax.axis_size("expert")
    nx = math.isqrt(dp)
    ny = dp // nx
    nz = ne // 2
    T, D = tokens.shape
    E, _, F = gate_weight.shape
    e_total = E * ne
    rows = 2 * nz * T
    d = lax.axis_index("dp")
    e = lax.axis_index("expert")
    xi, yi, ci = d % nx, d // nx, e % 2

    z_groups = [[2 * z + c for z in range(nz)] for c in range(2)]
    swap_pairs = [(i, i ^ 1) for i in range(ne)]

    def shift_x(k):
        return [(y * nx + x, y * nx + (x + k) % nx) for y in range(ny) for x in range(nx)]

    def shift_y(k):
        return [(y * nx + x, ((y + k) % ny) * nx + x) for y in range(ny) for x in range(nx)]

    def swap(v):
        return lax.ppermute(v, "expert", swap_pairs)

    def over_z(v):
        return lax.all_to_all(
            v, "expert", split_axis=0, concat_axis=0, tiled=True, axis_index_groups=z_groups
        )

    def gather_rows(v):
        near = over_z(jnp.broadcast_to(v[None], (nz, T, D)))
        return near, swap(near)

    def return_rows(part):
        near = part[: nz * T] + swap(part[nz * T :].astype(BF)).astype(F32)
        return jnp.sum(over_z(near.astype(BF).reshape(nz, T, D)).astype(F32), axis=0).astype(BF)

    def own_first(v):
        return jnp.where(ci == 0, v, v[:, ::-1])

    hot = (routes[:, :, None] == jnp.arange(e_total, dtype=jnp.int32)).astype(F32)
    weights = jnp.einsum("tk,tke->et", route_weights, hot, precision="highest")
    weights = lax.all_to_all(
        weights.reshape(ne, E, T), "expert", split_axis=0, concat_axis=0, tiled=True
    )
    weights = own_first(weights.reshape(nz, 2, E, T)).transpose(2, 1, 0, 3).reshape(E, rows, 1)

    token_rows = jnp.concatenate(gather_rows(tokens)).reshape(rows, D)
    cot_rows = jnp.concatenate(gather_rows(cotangent)).reshape(rows, D)

    def dot(spec, a, b):
        return jnp.einsum(spec, a, b, preferred_element_type=F32)

    gate_pre = dot("td,edf->etf", token_rows, gate_weight)
    up_pre = dot("td,edf->etf", token_rows, up_weight)
    sig = jax.nn.sigmoid(gate_pre)
    silu = gate_pre * sig
    hidden = silu * up_pre
    scaled = (weights * hidden).astype(BF)
    layer_out = return_rows(dot("etf,efd->td", scaled, down_weight))

    down_part = dot("etf,td->efd", scaled, cot_rows)
    hidden_grad = dot("td,efd->etf", cot_rows, down_weight)
    route_part = jnp.sum(hidden * hidden_grad, axis=2)
    weighted = weights * hidden_grad
    gate_grad = (weighted * up_pre * sig * (1.0 + gate_pre * (1.0 - sig))).astype(BF)
    up_grad = (weighted * silu).astype(BF)
    gate_part = dot("td,etf->edf", token_rows, gate_grad)
    up_part = dot("td,etf->edf", token_rows, up_grad)
    token_grads = return_rows(
        dot("etf,edf->td", gate_grad, gate_weight) + dot("etf,edf->td", up_grad, up_weight)
    )

    route_part = own_first(route_part.reshape(E, 2, nz, T).transpose(2, 1, 0, 3))
    route_all = lax.all_to_all(
        route_part.reshape(ne, E, T), "expert", split_axis=0, concat_axis=0, tiled=True
    ).reshape(e_total, T)
    route_grads = jnp.einsum("et,tke->tk", route_all, hot, precision="highest")

    def reduce_axis(v, axis, i, n, pairs):
        total = pick(v, i, axis)
        for k in range(1, n):
            sent = pick(v, (i + k) % n, axis).astype(BF)
            total = total + lax.ppermute(sent, "dp", pairs(k)).astype(F32)
        return total

    def reduce_dp(part):
        r = part.shape[1] // dp
        done = []
        for j in range(E):
            v = part[j].reshape(ny, nx, r, part.shape[2])
            if j % 2 == 0:
                v = reduce_axis(v, 1, xi, nx, shift_x)
                v = reduce_axis(v, 0, yi, ny, shift_y)
            else:
                v = reduce_axis(v, 0, yi, ny, shift_y)
                v = reduce_axis(v, 0, xi, nx, shift_x)
            done.append(v)
        return jnp.stack(done)

    return (
        layer_out,
        token_grads,
        route_grads,
        reduce_dp(gate_part),
        reduce_dp(up_part),
        reduce_dp(down_part),
    )


def solution(mesh):
    rows = P(("dp", "expert"), None)
    weight = P("expert", None, None)
    grad = P("expert", "dp", None)
    return jax.shard_map(
        local,
        mesh=mesh,
        in_specs=(rows, rows, rows, weight, weight, weight, rows),
        out_specs=(rows, rows, rows, grad, grad, grad),
        check_vma=False,
    )
```

```python
import math

import jax
import jax.numpy as jnp
from jax import lax
from jax.experimental import pallas as pl
from jax.experimental.pallas import tpu as pltpu
from jax.sharding import PartitionSpec as P

BF = jnp.bfloat16
F32 = jnp.float32
VMEM = pl.BlockSpec(memory_space=pltpu.VMEM)
SMEM = pl.BlockSpec(memory_space=pltpu.SMEM)
NT = (((1,), (1,)), ((), ()))


def mm(a, b):
    return jnp.dot(a, b, preferred_element_type=F32)


def mm_nt(a, b):
    return lax.dot_general(a, b, NT, preferred_element_type=F32)


def size(s):
    return math.prod(s.shape) * jnp.dtype(s.dtype).itemsize


def on_chip(body, operands, out_shape, flops, name, scalars=0, scratch=()):
    total = sum(size(s) for s in list(operands) + list(out_shape))
    limit = min(60 * 2**20, total // 3 + sum(size(s) for s in scratch) + 4 * 2**20)
    return pl.pallas_call(
        body,
        in_specs=[SMEM] * scalars + [VMEM] * (len(operands) - scalars),
        out_specs=[VMEM] * len(out_shape),
        out_shape=out_shape,
        scratch_shapes=list(scratch),
        compiler_params=pltpu.CompilerParams(vmem_limit_bytes=limit),
        cost_estimate=pl.CostEstimate(
            flops=10**10, bytes_accessed=total, transcendentals=0
        ),
        name=name,
    )(*operands)


def extra_rows(e_total, T, D):
    return -(-3 * e_total * T // (8 * D)) * 8


def thirds(v):
    hi = v.astype(BF).astype(F32)
    mid = (v - hi).astype(BF).astype(F32)
    return hi, mid, v - hi - mid


def pack_tokens(tokens, routes_t, weights_t, e_total):
    T, D = tokens.shape
    extra = extra_rows(e_total, T, D)
    per = D // T

    def body(tok_ref, routes_ref, weights_ref, out_ref, buf):
        expert = lax.broadcasted_iota(jnp.int32, (e_total, T), 0)
        dense = jnp.zeros((e_total, T), F32)
        for k in range(routes_t.shape[0]):
            dense = dense + jnp.where(
                routes_ref[k : k + 1, :] == expert, weights_ref[k : k + 1, :], 0.0
            )
        buf[...] = jnp.zeros_like(buf)
        for p, part in enumerate(thirds(dense)):
            for i in range(e_total):
                row = p * (e_total // per) + i // per
                at = slice(i % per * T, (i % per + 1) * T)
                buf[row : row + 1, at] = part[i : i + 1, :]
        out_ref[:T, :] = tok_ref[...]
        out_ref[T:, :] = buf[...].astype(BF)

    return on_chip(
        body,
        [tokens, routes_t, weights_t],
        [jax.ShapeDtypeStruct((T + extra, D), BF)],
        0,
        "pack_tokens",
        scratch=[pltpu.VMEM((extra, D), F32)],
    )[0]


def collect(blocks, *earlier):
    nb, h = len(blocks), blocks[0].shape[0]

    def body(*refs):
        for i in range(nb):
            refs[-1][i * h : (i + 1) * h, :] = refs[i][...]

    shape = jax.ShapeDtypeStruct((nb * h, blocks[0].shape[1]), BF)
    return on_chip(body, [*blocks, *earlier], [shape], 0, "collect")[0]


TOKEN = jax.ShapeDtypeStruct((8, 128), F32)


def forward(place, near, far, gate, up, down, T, e_total):
    E, D, F = gate.shape
    step = T + extra_rows(e_total, T, D)
    nb = near.shape[0] // step
    rows, wide, per = 2 * nb * T, E * F, e_total * T // D

    def body(place_ref, near_in, far_in, gate_ref, up_ref, down_ref, *refs):
        hid_refs, wa_refs, wb_refs = refs[0:2], refs[2:4], refs[4:6]
        hwt_ref, tokt_ref, near_ref, far_ref, token_ref, buf = refs[6:]
        token_ref[...] = jnp.zeros_like(token_ref)
        diagonal = lax.broadcasted_iota(jnp.int32, (T, T), 0) == lax.broadcasted_iota(
            jnp.int32, (T, T), 1
        )
        sublane = lax.broadcasted_iota(jnp.int32, (buf.shape[0], T), 0)
        buf[...] = jnp.zeros_like(buf)
        for side, source in enumerate((near_in, far_in)):
            for i in range(0, nb, 2):
                xs, ws = [], [[] for _ in range(E)]
                for b in (i, i + 1):
                    xs.append(source[b * step : b * step + T, :])
                    packed = source[b * step + T : (b + 1) * step, :].astype(F32)
                    buf[:per, :] = (
                        packed[:per] + packed[per : 2 * per] + packed[2 * per : 3 * per]
                    )
                    for j in range(E):
                        flat = (place_ref[2] * E + j) * T
                        at = pl.ds(pl.multiple_of(flat % D, T), T)
                        row = jnp.where(sublane == flat // D, buf[:, at], 0.0)
                        row = jnp.broadcast_to(jnp.sum(row, axis=0, keepdims=True), (T, T))
                        ws[j].append(
                            jnp.sum(jnp.where(diagonal, row, 0.0), axis=1, keepdims=True)
                        )
                x = jnp.concatenate(xs, axis=0)
                here = slice(i * T, (i + 2) * T)
                at = slice((side * nb + i) * T, (side * nb + i + 2) * T)
                tokt_ref[:, at] = x.T
                part = jnp.zeros((2 * T, D), F32)
                for j in range(E):
                    cols = slice(j * F, (j + 1) * F)
                    g = mm(x, gate_ref[j])
                    u = mm(x, up_ref[j])
                    w = jnp.concatenate(ws[j], axis=0)
                    s = jax.nn.sigmoid(g)
                    a = g * s
                    hid = a * u
                    hid_refs[side][here, cols] = hid.astype(BF)
                    wa_refs[side][here, cols] = (w * a).astype(BF)
                    wb_refs[side][here, cols] = (w * (u * s * (1.0 + g * (1.0 - s)))).astype(BF)
                    scaled = (w * hid).astype(BF)
                    hwt_ref[cols, at] = scaled.T
                    part = part + mm(scaled, down_ref[j])
                if side == 0:
                    near_ref[here, :] = part
                else:
                    far_ref[here, :] = part.astype(BF)

    out_shape = [jax.ShapeDtypeStruct((rows // 2, wide), BF)] * 6 + [
        jax.ShapeDtypeStruct((wide, rows), BF),
        jax.ShapeDtypeStruct((D, rows), BF),
        jax.ShapeDtypeStruct((rows // 2, D), F32),
        jax.ShapeDtypeStruct((rows // 2, D), BF),
        TOKEN,
    ]
    return on_chip(
        body,
        [place, near, far, gate, up, down],
        out_shape,
        6 * rows * D * wide,
        "forward",
        scalars=1,
        scratch=[pltpu.VMEM((-(-per // 8) * 8, D), F32)],
    )


def hidden_grads(cot, hid, wa, wb, down, *earlier):
    E, F, D = down.shape
    rows, wide = cot.shape[0], E * F
    step = 256

    def body(*refs):
        cot_ref, hid_ref, wa_ref, wb_ref, down_ref = refs[:5]
        gg_ref, ug_ref, rg_ref, token_ref = refs[5 + len(earlier) :]
        token_ref[...] = jnp.zeros_like(token_ref)
        lane = lax.broadcasted_iota(jnp.int32, (step, 128), 1)
        for m in range(0, rows, step):
            at = slice(m, m + step)
            c = cot_ref[at, :]
            total = jnp.zeros((step, 128), F32)
            for j in range(E):
                cols = slice(j * F, (j + 1) * F)
                h = mm_nt(c, down_ref[j])
                gg_ref[at, cols] = (h * wb_ref[at, cols].astype(F32)).astype(BF)
                ug_ref[at, cols] = (h * wa_ref[at, cols].astype(F32)).astype(BF)
                r = jnp.sum(h * hid_ref[at, cols].astype(F32), axis=1, keepdims=True)
                total = jnp.where(lane == j, r, total)
            rg_ref[at, :] = total

    out_shape = [jax.ShapeDtypeStruct((rows, wide), BF)] * 2 + [
        jax.ShapeDtypeStruct((rows, 128), F32),
        TOKEN,
    ]
    return on_chip(
        body,
        [cot, hid, wa, wb, down, *earlier],
        out_shape,
        2 * rows * D * wide,
        "hidden_grads",
    )


def token_partials(place, gg, ug, rg, gate, up, T, e_total, *earlier):
    half, wide = gg[0].shape
    E, D, F = gate.shape
    extra = extra_rows(e_total, T, D)
    step, nb, per = T + extra, half // T, e_total * T // D

    def body(*refs):
        place_ref = refs[0]
        gg_refs, ug_refs, rg_refs = refs[1:3], refs[3:5], refs[5:7]
        gate_ref, up_ref = refs[7:9]
        near_ref, far_ref, buf = refs[9 + len(earlier) :]
        sublane = lax.broadcasted_iota(jnp.int32, (extra, T), 0)
        for side in range(2):
            for i in range(0, nb, 2):
                at = slice(i * T, (i + 2) * T)
                part = jnp.zeros((2 * T, D), F32)
                for j in range(E):
                    cols = slice(j * F, (j + 1) * F)
                    part = part + mm_nt(gg_refs[side][at, cols], gate_ref[j])
                    part = part + mm_nt(ug_refs[side][at, cols], up_ref[j])
                for b in (i, i + 1):
                    buf[...] = jnp.zeros_like(buf)
                    turned = rg_refs[side][b * T : (b + 1) * T, :].T
                    for p, third in enumerate(thirds(turned[:8, :])):
                        for j in range(E):
                            flat = (place_ref[2] * E + j) * T
                            lanes = pl.ds(pl.multiple_of(flat % D, T), T)
                            mine = jnp.broadcast_to(third[j : j + 1, :], (extra, T))
                            row = sublane == p * per + flat // D
                            buf[:, lanes] = jnp.where(row, mine, buf[:, lanes])
                    mine = part[(b - i) * T : (b - i + 1) * T]
                    if side == 0:
                        near_ref[b * step : b * step + T, :] = mine
                        near_ref[b * step + T : (b + 1) * step, :] = buf[...]
                    else:
                        far_ref[b * step : b * step + T, :] = mine.astype(BF)
                        far_ref[b * step + T : (b + 1) * step, :] = buf[...].astype(BF)

    out_shape = [
        jax.ShapeDtypeStruct((nb * step, D), F32),
        jax.ShapeDtypeStruct((nb * step, D), BF),
    ]
    return on_chip(
        body,
        [place, *gg, *ug, *rg, gate, up, *earlier],
        out_shape,
        8 * half * D * wide,
        "token_partials",
        scalars=1,
        scratch=[pltpu.VMEM((extra, D), F32)],
    )


def weight_partials(place, lhs_t, rhs, experts, n, out_rows, name, *earlier):
    r = out_rows // (n * n)
    rows = lhs_t.shape[1]
    half = rows // 2
    joined = lhs_t.shape[0] != out_rows
    width = rhs[0].shape[1] // (1 if joined else experts)
    per = n * n if joined else 0

    def body(place_ref, left_ref, *refs):
        xi, yi = place_ref[0], place_ref[1]
        outs = refs[2 + len(earlier) : -1]
        refs[-1][...] = jnp.zeros_like(refs[-1])
        for k in [*range(1, n), 0]:
            for j in range(experts):
                left = []
                for q in range(n):
                    a, b = (k, q) if j % 2 == 0 else (q, k)
                    block = j * per + ((yi + b) % n) * n + (xi + a) % n
                    left.append(left_ref[pl.ds(pl.multiple_of(block * r, r), r), :])
                left = jnp.concatenate(left, axis=0)
                cols = slice(0, width) if joined else slice(j * width, (j + 1) * width)
                part = mm(left[:, :half], refs[0][:, cols]) + mm(left[:, half:], refs[1][:, cols])
                part = part.reshape(n, r, width)
                if k:
                    outs[2 * j][k - 1] = part.astype(BF)
                else:
                    outs[2 * j + 1][...] = part

    out_shape = [
        jax.ShapeDtypeStruct((n - 1, n, r, width), BF),
        jax.ShapeDtypeStruct((n, r, width), F32),
    ] * experts + [TOKEN]
    outs = on_chip(
        body,
        [place, lhs_t, *rhs, *earlier],
        out_shape,
        2 * experts * out_rows * width * rows,
        name,
        scalars=1,
    )
    return [(outs[2 * j], outs[2 * j + 1]) for j in range(experts)], outs[-1]


def add_first(parts, got, n, name, *earlier):
    E = len(parts)
    _, r, width = parts[0][1].shape

    def body(*refs):
        ins, outs = refs[: E * n], refs[E * n + len(earlier) :]
        outs[-1][...] = jnp.zeros_like(outs[-1])
        for j in range(E):
            for q in range(n):
                total = ins[j * n][q]
                for k in range(1, n):
                    total = total + ins[j * n + k][q].astype(F32)
                out = outs[j * n + q]
                out[...] = total.astype(out.dtype)

    operands = [v for j in range(E) for v in (parts[j][1], *got[j])]
    shapes = [jax.ShapeDtypeStruct((r, width), F32 if q == 0 else BF) for q in range(n)] * E
    outs = on_chip(body, [*operands, *earlier], shapes + [TOKEN], 0, name)
    return [outs[j * n : (j + 1) * n] for j in range(E)], outs[-1]


def add_second(totals, got, n, name, *earlier):
    E = len(totals)
    r, width = totals[0][0].shape

    def body(*refs):
        ins, (out_ref, token_ref) = refs[: E * n], refs[E * n + len(earlier) :]
        token_ref[...] = jnp.zeros_like(token_ref)
        for j in range(E):
            total = ins[j * n][...]
            for k in range(1, n):
                total = total + ins[j * n + k][...].astype(F32)
            out_ref[j] = total

    operands = [v for j in range(E) for v in (totals[j][0], *got[j])]
    return on_chip(
        body,
        [*operands, *earlier],
        [jax.ShapeDtypeStruct((E, r, width), F32), TOKEN],
        0,
        name,
    )


def add_sides(place, near, far, nz, name, *earlier):
    step, D = near.shape[0] // nz, near.shape[1]

    def body(place_ref, near_ref, far_ref, *refs):
        out_ref, token_ref = refs[len(earlier) :]
        token_ref[...] = jnp.zeros_like(token_ref)
        z = place_ref[2] // 2
        for k in range(nz):
            at = slice(k * step, (k + 1) * step)
            total = near_ref[at, :] + far_ref[at, :].astype(F32)
            to = pl.multiple_of((z - k + nz) % nz * step, step)
            out_ref[pl.ds(to, step), :] = total.astype(BF)

    shapes = [jax.ShapeDtypeStruct((nz * step, D), BF), TOKEN]
    return on_chip(body, [place, near, far, *earlier], shapes, 0, name, scalars=1)


def split_sides(near, far, nz, name, *earlier):
    step, D = near.shape[0] // nz, near.shape[1]

    def body(near_ref, far_ref, *refs):
        outs = refs[len(earlier) :]
        for k in range(nz):
            at = slice(k * step, (k + 1) * step)
            total = near_ref[at, :] + far_ref[at, :].astype(F32)
            outs[k][...] = total.astype(outs[k].dtype)

    shapes = [jax.ShapeDtypeStruct((step, D), F32 if k == 0 else BF) for k in range(nz)]
    return on_chip(body, [near, far, *earlier], shapes, 0, name)


def sum_rows(own, got, name, *earlier):
    def body(*refs):
        total = refs[0][...]
        for g in refs[1 : 1 + len(got)]:
            total = total + g[...].astype(F32)
        refs[-2][...] = total.astype(BF)
        refs[-1][...] = jnp.zeros_like(refs[-1])

    shapes = [jax.ShapeDtypeStruct(own.shape, BF), TOKEN]
    return on_chip(body, [own, *got, *earlier], shapes, 0, name)


def sum_rows_and_routes(got, routes_t, nz, e_total, name):
    top, T = routes_t.shape
    step, D = got.shape[0] // nz, got.shape[1]
    per, lanes = e_total * T // D, D // T

    def body(*refs):
        routes_ref, got_ref, rows_ref, routes_out, token_ref = refs
        token_ref[...] = jnp.zeros_like(token_ref)
        total = got_ref[:step, :].astype(F32)
        for k in range(1, nz):
            total = total + got_ref[k * step : (k + 1) * step, :].astype(F32)
        rows_ref[...] = total[:T].astype(BF)
        packed = total[T:]
        packed = packed[:per] + packed[per : 2 * per] + packed[2 * per : 3 * per]
        grads = jnp.zeros((top, T), F32)
        for i in range(e_total):
            at = slice(i % lanes * T, (i % lanes + 1) * T)
            row = packed[i // lanes : i // lanes + 1, at]
            grads = jnp.where(routes_ref[...] == i, row, grads)
        routes_out[...] = grads

    shapes = [
        jax.ShapeDtypeStruct((T, D), BF),
        jax.ShapeDtypeStruct((top, T), F32),
        TOKEN,
    ]
    return on_chip(body, [routes_t, got], shapes, 0, name)


def local(tokens, routes, route_weights, gate_weight, up_weight, down_weight, cotangent):
    dp = lax.axis_size("dp")
    ne = lax.axis_size("expert")
    n = math.isqrt(dp)
    nz = ne // 2
    T, D = tokens.shape
    E, _, F = gate_weight.shape
    e_total = E * ne
    d = lax.axis_index("dp")
    e = lax.axis_index("expert")
    place = jnp.stack([d % n, d // n, e]).astype(jnp.int32)

    def swap(v):
        return lax.ppermute(v, "expert", [(i, i ^ 1) for i in range(ne)])

    def move_z(v, k):
        pairs = [(2 * z + c, 2 * ((z + k) % nz) + c) for z in range(nz) for c in range(2)]
        return lax.ppermute(v, "expert", pairs)

    def move_x(v, k):
        pairs = [(y * n + x, y * n + (x + k) % n) for y in range(n) for x in range(n)]
        return lax.ppermute(v, "dp", pairs)

    def move_y(v, k):
        pairs = [(y * n + x, ((y + k) % n) * n + x) for y in range(n) for x in range(n)]
        return lax.ppermute(v, "dp", pairs)

    def gather_near(v):
        return [v] + [move_z(v, k) for k in range(1, nz)]

    packed = pack_tokens(tokens, routes.T, route_weights.T, e_total)
    token_near = collect(gather_near(packed))
    cot_blocks = gather_near(cotangent)
    token_far = swap(token_near)
    *saved, hw_t, tok_t, out_near, out_far, forward_done = forward(
        place, token_near, token_far, gate_weight, up_weight, down_weight, T, e_total
    )
    hid, wa, wb = saved[0:2], saved[2:4], saved[4:6]
    out_far = swap(out_far)
    cot_near = collect(cot_blocks, forward_done)
    cot_far = swap(cot_near)

    def send_first(parts):
        got = []
        for j, (sent, _) in enumerate(parts):
            move = move_x if j % 2 == 0 else move_y
            got.append([move(sent[k - 1], k) for k in range(1, n)])
        return got

    def send_second(totals):
        got = []
        for j, total in enumerate(totals):
            move = move_y if j % 2 == 0 else move_x
            got.append([move(total[k], k) for k in range(1, n)])
        return got

    z_groups = [[2 * z + c for z in range(nz)] for c in range(2)]

    def send_home(parts):
        return lax.all_to_all(
            parts,
            "expert",
            split_axis=0,
            concat_axis=0,
            tiled=True,
            axis_index_groups=z_groups,
        )

    gg0, ug0, rg0, near_done = hidden_grads(cot_near, hid[0], wa[0], wb[0], down_weight)
    down_part, down_done = weight_partials(
        place, hw_t, [cot_near, cot_far], E, n, F, "down_partials", near_done
    )
    down_got = send_first(down_part)
    gg1, ug1, rg1, _ = hidden_grads(cot_far, hid[1], wa[1], wb[1], down_weight, down_done)
    gate_part, gate_done = weight_partials(place, tok_t, [gg0, gg1], E, n, D, "gate_partials")
    gate_got = send_first(gate_part)
    out_parts = split_sides(out_near, out_far, nz, "out_sides", down_done)
    out_got = [move_z(out_parts[k], -k) for k in range(1, nz)]
    down_totals, down_mid = add_first(down_part, down_got, n, "down_first", gate_done)
    tg_near, tg_far = token_partials(
        place,
        [gg0, gg1],
        [ug0, ug1],
        [rg0, rg1],
        gate_weight,
        up_weight,
        T,
        e_total,
        down_mid,
    )
    tg_far = swap(tg_far)
    layer_out, out_done = sum_rows(out_parts[0], out_got, "out_rows", tg_near[:8, :128])
    up_part, up_done = weight_partials(
        place, tok_t, [ug0, ug1], E, n, D, "up_partials", tg_near[:8, :128], out_done
    )
    up_got = send_first(up_part)
    down_got = send_second(down_totals)
    tg_parts, tg_done = add_sides(place, tg_near, tg_far, nz, "token_sides", up_done)
    tg_got = send_home(tg_parts)
    gate_totals, gate_mid = add_first(gate_part, gate_got, n, "gate_first", tg_done)
    gate_got = send_second(gate_totals)
    up_totals, up_mid = add_first(up_part, up_got, n, "up_first", gate_mid)
    up_got = send_second(up_totals)
    down_grads, down_done = add_second(down_totals, down_got, n, "down_second", up_mid)
    gate_grads, gate_done = add_second(gate_totals, gate_got, n, "gate_second", down_done)
    token_grads, route_grads_t, rows_done = sum_rows_and_routes(
        tg_got, routes.T, nz, e_total, "token_rows"
    )
    up_grads, _ = add_second(up_totals, up_got, n, "up_second", gate_done, rows_done)
    route_grads = route_grads_t.T

    return (layer_out, token_grads, route_grads, gate_grads, up_grads, down_grads)


def solution(mesh):
    rows = P(("dp", "expert"), None)
    weight = P("expert", None, None)
    grad = P("expert", "dp", None)
    return jax.shard_map(
        local,
        mesh=mesh,
        in_specs=(rows, rows, rows, weight, weight, weight, rows),
        out_specs=(rows, rows, rows, grad, grad, grad),
        check_vma=False,
    )
```

```python
import math

import jax
import jax.numpy as jnp
from jax import lax
from jax.experimental import pallas as pl
from jax.experimental.pallas import tpu as pltpu
from jax.sharding import PartitionSpec as P

BF = jnp.bfloat16
F32 = jnp.float32
VMEM = pl.BlockSpec(memory_space=pltpu.VMEM)
SMEM = pl.BlockSpec(memory_space=pltpu.SMEM)
NT = (((1,), (1,)), ((), ()))


def mm(a, b):
    return jnp.dot(a, b, preferred_element_type=F32)


def mm_nt(a, b):
    return lax.dot_general(a, b, NT, preferred_element_type=F32)


def size(s):
    return math.prod(s.shape) * jnp.dtype(s.dtype).itemsize


def on_chip(body, operands, out_shape, flops, name, scalars=0, scratch=()):
    total = sum(size(s) for s in list(operands) + list(out_shape))
    limit = min(60 * 2**20, total // 3 + sum(size(s) for s in scratch) + 4 * 2**20)
    return pl.pallas_call(
        body,
        in_specs=[SMEM] * scalars + [VMEM] * (len(operands) - scalars),
        out_specs=[VMEM] * len(out_shape),
        out_shape=out_shape,
        scratch_shapes=list(scratch),
        compiler_params=pltpu.CompilerParams(vmem_limit_bytes=limit),
        cost_estimate=pl.CostEstimate(
            flops=10**10, bytes_accessed=total, transcendentals=0
        ),
        name=name,
    )(*operands)


def extra_rows(e_total, T, D):
    return -(-3 * e_total * T // (8 * D)) * 8


def thirds(v):
    hi = v.astype(BF).astype(F32)
    mid = (v - hi).astype(BF).astype(F32)
    return hi, mid, v - hi - mid


def pack_tokens(tokens, routes_t, weights_t, e_total):
    T, D = tokens.shape
    extra = extra_rows(e_total, T, D)
    per = D // T

    def body(tok_ref, routes_ref, weights_ref, out_ref, buf):
        expert = lax.broadcasted_iota(jnp.int32, (e_total, T), 0)
        dense = jnp.zeros((e_total, T), F32)
        for k in range(routes_t.shape[0]):
            dense = dense + jnp.where(
                routes_ref[k : k + 1, :] == expert, weights_ref[k : k + 1, :], 0.0
            )
        buf[...] = jnp.zeros_like(buf)
        for p, part in enumerate(thirds(dense)):
            for i in range(e_total):
                row = p * (e_total // per) + i // per
                at = slice(i % per * T, (i % per + 1) * T)
                buf[row : row + 1, at] = part[i : i + 1, :]
        out_ref[:T, :] = tok_ref[...]
        out_ref[T:, :] = buf[...].astype(BF)

    return on_chip(
        body,
        [tokens, routes_t, weights_t],
        [jax.ShapeDtypeStruct((T + extra, D), BF)],
        0,
        "pack_tokens",
        scratch=[pltpu.VMEM((extra, D), F32)],
    )[0]


def collect(blocks, *earlier):
    nb, h = len(blocks), blocks[0].shape[0]

    def body(*refs):
        for i in range(nb):
            refs[-1][i * h : (i + 1) * h, :] = refs[i][...]

    shape = jax.ShapeDtypeStruct((nb * h, blocks[0].shape[1]), BF)
    return on_chip(body, [*blocks, *earlier], [shape], 0, "collect")[0]


TOKEN = jax.ShapeDtypeStruct((8, 128), F32)


def forward(place, near, far, gate, up, down, T, e_total):
    E, D, F = gate.shape
    step = T + extra_rows(e_total, T, D)
    nb = near.shape[0] // step
    rows, wide, per = 2 * nb * T, E * F, e_total * T // D

    def body(place_ref, near_in, far_in, gate_ref, up_ref, down_ref, *refs):
        hid_refs, wa_refs, wb_refs = refs[0:2], refs[2:4], refs[4:6]
        hwt_ref, tokt_ref, near_ref, far_ref, token_ref, buf = refs[6:]
        token_ref[...] = jnp.zeros_like(token_ref)
        diagonal = lax.broadcasted_iota(jnp.int32, (T, T), 0) == lax.broadcasted_iota(
            jnp.int32, (T, T), 1
        )
        sublane = lax.broadcasted_iota(jnp.int32, (buf.shape[0], T), 0)
        buf[...] = jnp.zeros_like(buf)
        for side, source in enumerate((near_in, far_in)):
            for i in range(0, nb, 2):
                xs, ws = [], [[] for _ in range(E)]
                for b in (i, i + 1):
                    xs.append(source[b * step : b * step + T, :])
                    packed = source[b * step + T : (b + 1) * step, :].astype(F32)
                    buf[:per, :] = (
                        packed[:per] + packed[per : 2 * per] + packed[2 * per : 3 * per]
                    )
                    for j in range(E):
                        flat = (place_ref[2] * E + j) * T
                        at = pl.ds(pl.multiple_of(flat % D, T), T)
                        row = jnp.where(sublane == flat // D, buf[:, at], 0.0)
                        row = jnp.broadcast_to(jnp.sum(row, axis=0, keepdims=True), (T, T))
                        ws[j].append(
                            jnp.sum(jnp.where(diagonal, row, 0.0), axis=1, keepdims=True)
                        )
                x = jnp.concatenate(xs, axis=0)
                here = slice(i * T, (i + 2) * T)
                at = slice((side * nb + i) * T, (side * nb + i + 2) * T)
                tokt_ref[:, at] = x.T
                part = jnp.zeros((2 * T, D), F32)
                for j in range(E):
                    cols = slice(j * F, (j + 1) * F)
                    g = mm(x, gate_ref[j])
                    u = mm(x, up_ref[j])
                    w = jnp.concatenate(ws[j], axis=0)
                    s = jax.nn.sigmoid(g)
                    a = g * s
                    hid = a * u
                    hid_refs[side][here, cols] = hid.astype(BF)
                    wa_refs[side][here, cols] = (w * a).astype(BF)
                    wb_refs[side][here, cols] = (w * (u * s * (1.0 + g * (1.0 - s)))).astype(BF)
                    scaled = (w * hid).astype(BF)
                    hwt_ref[cols, at] = scaled.T
                    part = part + mm(scaled, down_ref[j])
                if side == 0:
                    near_ref[here, :] = part
                else:
                    far_ref[here, :] = part.astype(BF)

    out_shape = [jax.ShapeDtypeStruct((rows // 2, wide), BF)] * 6 + [
        jax.ShapeDtypeStruct((wide, rows), BF),
        jax.ShapeDtypeStruct((D, rows), BF),
        jax.ShapeDtypeStruct((rows // 2, D), F32),
        jax.ShapeDtypeStruct((rows // 2, D), BF),
        TOKEN,
    ]
    return on_chip(
        body,
        [place, near, far, gate, up, down],
        out_shape,
        6 * rows * D * wide,
        "forward",
        scalars=1,
        scratch=[pltpu.VMEM((-(-per // 8) * 8, D), F32)],
    )


def hidden_grads(cot, hid, wa, wb, down, *earlier):
    E, F, D = down.shape
    rows, wide = cot.shape[0], E * F
    step = 256

    def body(*refs):
        cot_ref, hid_ref, wa_ref, wb_ref, down_ref = refs[:5]
        gg_ref, ug_ref, rg_ref, token_ref = refs[5 + len(earlier) :]
        token_ref[...] = jnp.zeros_like(token_ref)
        lane = lax.broadcasted_iota(jnp.int32, (step, 128), 1)
        for m in range(0, rows, step):
            at = slice(m, m + step)
            c = cot_ref[at, :]
            total = jnp.zeros((step, 128), F32)
            for j in range(E):
                cols = slice(j * F, (j + 1) * F)
                h = mm_nt(c, down_ref[j])
                gg_ref[at, cols] = (h * wb_ref[at, cols].astype(F32)).astype(BF)
                ug_ref[at, cols] = (h * wa_ref[at, cols].astype(F32)).astype(BF)
                r = jnp.sum(h * hid_ref[at, cols].astype(F32), axis=1, keepdims=True)
                total = jnp.where(lane == j, r, total)
            rg_ref[at, :] = total

    out_shape = [jax.ShapeDtypeStruct((rows, wide), BF)] * 2 + [
        jax.ShapeDtypeStruct((rows, 128), F32),
        TOKEN,
    ]
    return on_chip(
        body,
        [cot, hid, wa, wb, down, *earlier],
        out_shape,
        2 * rows * D * wide,
        "hidden_grads",
    )


def token_partials(place, gg, ug, rg, gate, up, T, e_total, *earlier):
    half, wide = gg[0].shape
    E, D, F = gate.shape
    extra = extra_rows(e_total, T, D)
    step, nb, per = T + extra, half // T, e_total * T // D

    def body(*refs):
        place_ref = refs[0]
        gg_refs, ug_refs, rg_refs = refs[1:3], refs[3:5], refs[5:7]
        gate_ref, up_ref = refs[7:9]
        near_ref, far_ref, buf = refs[9 + len(earlier) :]
        sublane = lax.broadcasted_iota(jnp.int32, (extra, T), 0)
        for side in range(2):
            for i in range(0, nb, 2):
                at = slice(i * T, (i + 2) * T)
                part = jnp.zeros((2 * T, D), F32)
                for j in range(E):
                    cols = slice(j * F, (j + 1) * F)
                    part = part + mm_nt(gg_refs[side][at, cols], gate_ref[j])
                    part = part + mm_nt(ug_refs[side][at, cols], up_ref[j])
                for b in (i, i + 1):
                    buf[...] = jnp.zeros_like(buf)
                    turned = rg_refs[side][b * T : (b + 1) * T, :].T
                    for p, third in enumerate(thirds(turned[:8, :])):
                        for j in range(E):
                            flat = (place_ref[2] * E + j) * T
                            lanes = pl.ds(pl.multiple_of(flat % D, T), T)
                            mine = jnp.broadcast_to(third[j : j + 1, :], (extra, T))
                            row = sublane == p * per + flat // D
                            buf[:, lanes] = jnp.where(row, mine, buf[:, lanes])
                    mine = part[(b - i) * T : (b - i + 1) * T]
                    if side == 0:
                        near_ref[b * step : b * step + T, :] = mine
                        near_ref[b * step + T : (b + 1) * step, :] = buf[...]
                    else:
                        far_ref[b * step : b * step + T, :] = mine.astype(BF)
                        far_ref[b * step + T : (b + 1) * step, :] = buf[...].astype(BF)

    out_shape = [
        jax.ShapeDtypeStruct((nb * step, D), F32),
        jax.ShapeDtypeStruct((nb * step, D), BF),
    ]
    return on_chip(
        body,
        [place, *gg, *ug, *rg, gate, up, *earlier],
        out_shape,
        8 * half * D * wide,
        "token_partials",
        scalars=1,
        scratch=[pltpu.VMEM((extra, D), F32)],
    )


def weight_partials(place, lhs_t, rhs, experts, n, out_rows, name, *earlier):
    r = out_rows // (n * n)
    rows = lhs_t.shape[1]
    half = rows // 2
    joined = lhs_t.shape[0] != out_rows
    width = rhs[0].shape[1] // (1 if joined else experts)
    per = n * n if joined else 0

    def body(place_ref, left_ref, *refs):
        xi, yi = place_ref[0], place_ref[1]
        outs = refs[2 + len(earlier) : -1]
        refs[-1][...] = jnp.zeros_like(refs[-1])
        for k in [*range(1, n), 0]:
            for j in range(experts):
                left = []
                for q in range(n):
                    a, b = (k, q) if j % 2 == 0 else (q, k)
                    block = j * per + ((yi + b) % n) * n + (xi + a) % n
                    left.append(left_ref[pl.ds(pl.multiple_of(block * r, r), r), :])
                left = jnp.concatenate(left, axis=0)
                cols = slice(0, width) if joined else slice(j * width, (j + 1) * width)
                part = mm(left[:, :half], refs[0][:, cols]) + mm(left[:, half:], refs[1][:, cols])
                part = part.reshape(n, r, width)
                if k:
                    outs[2 * j][k - 1] = part.astype(BF)
                else:
                    outs[2 * j + 1][...] = part

    out_shape = [
        jax.ShapeDtypeStruct((n - 1, n, r, width), BF),
        jax.ShapeDtypeStruct((n, r, width), F32),
    ] * experts + [TOKEN]
    outs = on_chip(
        body,
        [place, lhs_t, *rhs, *earlier],
        out_shape,
        2 * experts * out_rows * width * rows,
        name,
        scalars=1,
    )
    return [(outs[2 * j], outs[2 * j + 1]) for j in range(experts)], outs[-1]


def add_first(parts, got, n, name, *earlier):
    E = len(parts)
    _, r, width = parts[0][1].shape

    def body(*refs):
        ins, outs = refs[: E * n], refs[E * n + len(earlier) :]
        outs[-1][...] = jnp.zeros_like(outs[-1])
        for j in range(E):
            for q in range(n):
                total = ins[j * n][q]
                for k in range(1, n):
                    total = total + ins[j * n + k][q].astype(F32)
                out = outs[j * n + q]
                out[...] = total.astype(out.dtype)

    operands = [v for j in range(E) for v in (parts[j][1], *got[j])]
    shapes = [jax.ShapeDtypeStruct((r, width), F32 if q == 0 else BF) for q in range(n)] * E
    outs = on_chip(body, [*operands, *earlier], shapes + [TOKEN], 0, name)
    return [outs[j * n : (j + 1) * n] for j in range(E)], outs[-1]


def relay(totals, name, *earlier):
    sent = [v for total in totals for v in total[1:]]

    def body(*refs):
        outs = refs[len(sent) + len(earlier) :]
        outs[-1][...] = jnp.zeros_like(outs[-1])
        for source, out in zip(refs, outs[:-1]):
            out[...] = source[...]

    shapes = [jax.ShapeDtypeStruct(v.shape, v.dtype) for v in sent]
    *outs, done = on_chip(body, [*sent, *earlier], shapes + [TOKEN], 0, name)
    per = len(sent) // len(totals)
    return [[t[0], *outs[i * per : (i + 1) * per]] for i, t in enumerate(totals)], done


def add_second(totals, got, n, name, *earlier):
    E = len(totals)
    r, width = totals[0][0].shape

    def body(*refs):
        ins, (out_ref, token_ref) = refs[: E * n], refs[E * n + len(earlier) :]
        token_ref[...] = jnp.zeros_like(token_ref)
        for j in range(E):
            total = ins[j * n][...]
            for k in range(1, n):
                total = total + ins[j * n + k][...].astype(F32)
            out_ref[j] = total

    operands = [v for j in range(E) for v in (totals[j][0], *got[j])]
    return on_chip(
        body,
        [*operands, *earlier],
        [jax.ShapeDtypeStruct((E, r, width), F32), TOKEN],
        0,
        name,
    )


def add_sides(place, near, far, nz, name, *earlier):
    step, D = near.shape[0] // nz, near.shape[1]

    def body(place_ref, near_ref, far_ref, *refs):
        out_ref, token_ref = refs[len(earlier) :]
        token_ref[...] = jnp.zeros_like(token_ref)
        z = place_ref[2] // 2
        for k in range(nz):
            at = slice(k * step, (k + 1) * step)
            total = near_ref[at, :] + far_ref[at, :].astype(F32)
            to = pl.multiple_of((z - k + nz) % nz * step, step)
            out_ref[pl.ds(to, step), :] = total.astype(BF)

    shapes = [jax.ShapeDtypeStruct((nz * step, D), BF), TOKEN]
    return on_chip(body, [place, near, far, *earlier], shapes, 0, name, scalars=1)


def split_sides(near, far, nz, name, *earlier):
    step, D = near.shape[0] // nz, near.shape[1]

    def body(near_ref, far_ref, *refs):
        outs = refs[len(earlier) :]
        for k in range(nz):
            at = slice(k * step, (k + 1) * step)
            total = near_ref[at, :] + far_ref[at, :].astype(F32)
            outs[k][...] = total.astype(outs[k].dtype)

    shapes = [jax.ShapeDtypeStruct((step, D), F32 if k == 0 else BF) for k in range(nz)]
    return on_chip(body, [near, far, *earlier], shapes, 0, name)


def sum_rows(own, got, name, *earlier):
    def body(*refs):
        total = refs[0][...]
        for g in refs[1 : 1 + len(got)]:
            total = total + g[...].astype(F32)
        refs[-2][...] = total.astype(BF)
        refs[-1][...] = jnp.zeros_like(refs[-1])

    shapes = [jax.ShapeDtypeStruct(own.shape, BF), TOKEN]
    return on_chip(body, [own, *got, *earlier], shapes, 0, name)


def sum_rows_and_routes(got, routes_t, nz, e_total, name):
    top, T = routes_t.shape
    step, D = got.shape[0] // nz, got.shape[1]
    per, lanes = e_total * T // D, D // T

    def body(*refs):
        routes_ref, got_ref, rows_ref, routes_out, token_ref = refs
        token_ref[...] = jnp.zeros_like(token_ref)
        total = got_ref[:step, :].astype(F32)
        for k in range(1, nz):
            total = total + got_ref[k * step : (k + 1) * step, :].astype(F32)
        rows_ref[...] = total[:T].astype(BF)
        packed = total[T:]
        packed = packed[:per] + packed[per : 2 * per] + packed[2 * per : 3 * per]
        grads = jnp.zeros((top, T), F32)
        for i in range(e_total):
            at = slice(i % lanes * T, (i % lanes + 1) * T)
            row = packed[i // lanes : i // lanes + 1, at]
            grads = jnp.where(routes_ref[...] == i, row, grads)
        routes_out[...] = grads

    shapes = [
        jax.ShapeDtypeStruct((T, D), BF),
        jax.ShapeDtypeStruct((top, T), F32),
        TOKEN,
    ]
    return on_chip(body, [routes_t, got], shapes, 0, name)


def local(tokens, routes, route_weights, gate_weight, up_weight, down_weight, cotangent):
    dp = lax.axis_size("dp")
    ne = lax.axis_size("expert")
    n = math.isqrt(dp)
    nz = ne // 2
    T, D = tokens.shape
    E, _, F = gate_weight.shape
    e_total = E * ne
    d = lax.axis_index("dp")
    e = lax.axis_index("expert")
    place = jnp.stack([d % n, d // n, e]).astype(jnp.int32)

    def swap(v):
        return lax.ppermute(v, "expert", [(i, i ^ 1) for i in range(ne)])

    def move_z(v, k):
        pairs = [(2 * z + c, 2 * ((z + k) % nz) + c) for z in range(nz) for c in range(2)]
        return lax.ppermute(v, "expert", pairs)

    def move_x(v, k):
        pairs = [(y * n + x, y * n + (x + k) % n) for y in range(n) for x in range(n)]
        return lax.ppermute(v, "dp", pairs)

    def move_y(v, k):
        pairs = [(y * n + x, ((y + k) % n) * n + x) for y in range(n) for x in range(n)]
        return lax.ppermute(v, "dp", pairs)

    def gather_near(v):
        return [v] + [move_z(v, k) for k in range(1, nz)]

    packed = pack_tokens(tokens, routes.T, route_weights.T, e_total)
    token_near = collect(gather_near(packed))
    cot_blocks = gather_near(cotangent)
    token_far = swap(token_near)
    *saved, hw_t, tok_t, out_near, out_far, forward_done = forward(
        place, token_near, token_far, gate_weight, up_weight, down_weight, T, e_total
    )
    hid, wa, wb = saved[0:2], saved[2:4], saved[4:6]
    out_far = swap(out_far)
    cot_near = collect(cot_blocks, forward_done)
    cot_far = swap(cot_near)

    def send_first(parts):
        got = []
        for j, (sent, _) in enumerate(parts):
            move = move_x if j % 2 == 0 else move_y
            got.append([move(sent[k - 1], k) for k in range(1, n)])
        return got

    def send_second(totals):
        got = []
        for j, total in enumerate(totals):
            move = move_y if j % 2 == 0 else move_x
            got.append([move(total[k], k) for k in range(1, n)])
        return got

    z_groups = [[2 * z + c for z in range(nz)] for c in range(2)]

    def send_home(parts):
        return lax.all_to_all(
            parts,
            "expert",
            split_axis=0,
            concat_axis=0,
            tiled=True,
            axis_index_groups=z_groups,
        )

    gg0, ug0, rg0, near_done = hidden_grads(cot_near, hid[0], wa[0], wb[0], down_weight)
    down_part, down_done = weight_partials(
        place, hw_t, [cot_near, cot_far], E, n, F, "down_partials", near_done
    )
    down_got = send_first(down_part)
    gg1, ug1, rg1, _ = hidden_grads(cot_far, hid[1], wa[1], wb[1], down_weight, down_done)
    gate_part, gate_done = weight_partials(place, tok_t, [gg0, gg1], E, n, D, "gate_partials")
    gate_got = send_first(gate_part)
    out_parts = split_sides(out_near, out_far, nz, "out_sides", down_done)
    out_got = [move_z(out_parts[k], -k) for k in range(1, nz)]
    down_totals, down_mid = add_first(down_part, down_got, n, "down_first", gate_done)
    tg_near, tg_far = token_partials(
        place,
        [gg0, gg1],
        [ug0, ug1],
        [rg0, rg1],
        gate_weight,
        up_weight,
        T,
        e_total,
        down_mid,
    )
    tg_far = swap(tg_far)
    layer_out, out_done = sum_rows(out_parts[0], out_got, "out_rows", tg_near[:8, :128])
    up_part, up_done = weight_partials(
        place, tok_t, [ug0, ug1], E, n, D, "up_partials", tg_near[:8, :128], out_done
    )
    up_got = send_first(up_part)
    tg_parts, tg_done = add_sides(place, tg_near, tg_far, nz, "token_sides", up_done)
    tg_got = send_home(tg_parts)
    down_totals, down_mid = relay(down_totals, "down_relay", tg_done)
    down_got = send_second(down_totals)
    gate_totals, gate_mid = add_first(gate_part, gate_got, n, "gate_first", down_mid)
    gate_got = send_second(gate_totals)
    up_totals, up_mid = add_first(up_part, up_got, n, "up_first", gate_mid)
    up_got = send_second(up_totals)
    down_grads, down_done = add_second(down_totals, down_got, n, "down_second", up_mid)
    gate_grads, gate_done = add_second(gate_totals, gate_got, n, "gate_second", down_done)
    token_grads, route_grads_t, rows_done = sum_rows_and_routes(
        tg_got, routes.T, nz, e_total, "token_rows"
    )
    up_grads, _ = add_second(up_totals, up_got, n, "up_second", gate_done, rows_done)
    route_grads = route_grads_t.T

    return (layer_out, token_grads, route_grads, gate_grads, up_grads, down_grads)


def solution(mesh):
    rows = P(("dp", "expert"), None)
    weight = P("expert", None, None)
    grad = P("expert", "dp", None)
    return jax.shard_map(
        local,
        mesh=mesh,
        in_specs=(rows, rows, rows, weight, weight, weight, rows),
        out_specs=(rows, rows, rows, grad, grad, grad),
        check_vma=False,
    )
```

```python
import math

import jax
import jax.numpy as jnp
from jax import lax
from jax.experimental import pallas as pl
from jax.experimental.pallas import tpu as pltpu
from jax.sharding import PartitionSpec as P

BF = jnp.bfloat16
F32 = jnp.float32
VMEM = pl.BlockSpec(memory_space=pltpu.VMEM)
SMEM = pl.BlockSpec(memory_space=pltpu.SMEM)
NT = (((1,), (1,)), ((), ()))


def mm(a, b):
    return jnp.dot(a, b, preferred_element_type=F32)


def mm_nt(a, b):
    return lax.dot_general(a, b, NT, preferred_element_type=F32)


def size(s):
    return math.prod(s.shape) * jnp.dtype(s.dtype).itemsize


def on_chip(body, operands, out_shape, flops, name, scalars=0, scratch=()):
    total = sum(size(s) for s in list(operands) + list(out_shape))
    limit = min(60 * 2**20, total // 3 + sum(size(s) for s in scratch) + 4 * 2**20)
    return pl.pallas_call(
        body,
        in_specs=[SMEM] * scalars + [VMEM] * (len(operands) - scalars),
        out_specs=[VMEM] * len(out_shape),
        out_shape=out_shape,
        scratch_shapes=list(scratch),
        compiler_params=pltpu.CompilerParams(vmem_limit_bytes=limit),
        cost_estimate=pl.CostEstimate(
            flops=10**10, bytes_accessed=total, transcendentals=0
        ),
        name=name,
    )(*operands)


def extra_rows(e_total, T, D):
    return -(-3 * e_total * T // (8 * D)) * 8


def thirds(v):
    hi = v.astype(BF).astype(F32)
    mid = (v - hi).astype(BF).astype(F32)
    return hi, mid, v - hi - mid


def pack_tokens(tokens, routes_t, weights_t, e_total):
    T, D = tokens.shape
    extra = extra_rows(e_total, T, D)
    per = D // T

    def body(tok_hbm, routes_hbm, weights_hbm, out_ref, routes_ref, weights_ref, buf, sems):
        copies = [
            pltpu.make_async_copy(routes_hbm, routes_ref, sems.at[0]),
            pltpu.make_async_copy(weights_hbm, weights_ref, sems.at[1]),
            pltpu.make_async_copy(tok_hbm, out_ref.at[pl.ds(0, T)], sems.at[2]),
        ]
        for c in copies:
            c.start()
        buf[...] = jnp.zeros_like(buf)
        expert = lax.broadcasted_iota(jnp.int32, (e_total, T), 0)
        dense = jnp.zeros((e_total, T), F32)
        copies[0].wait()
        copies[1].wait()
        for k in range(routes_t.shape[0]):
            dense = dense + jnp.where(
                routes_ref[k : k + 1, :] == expert, weights_ref[k : k + 1, :], 0.0
            )
        for p, part in enumerate(thirds(dense)):
            for i in range(e_total):
                row = p * (e_total // per) + i // per
                at = slice(i % per * T, (i % per + 1) * T)
                buf[row : row + 1, at] = part[i : i + 1, :]
        out_ref[T:, :] = buf[...].astype(BF)
        copies[2].wait()

    return pl.pallas_call(
        body,
        in_specs=[pl.BlockSpec(memory_space=pl.ANY)] * 3,
        out_specs=VMEM,
        out_shape=jax.ShapeDtypeStruct((T + extra, D), BF),
        scratch_shapes=[
            pltpu.VMEM(routes_t.shape, jnp.int32),
            pltpu.VMEM(weights_t.shape, F32),
            pltpu.VMEM((extra, D), F32),
            pltpu.SemaphoreType.DMA((3,)),
        ],
        compiler_params=pltpu.CompilerParams(vmem_limit_bytes=60 * 2**20),
        cost_estimate=pl.CostEstimate(flops=10**10, bytes_accessed=2**20, transcendentals=0),
        name="pack_tokens",
    )(tokens, routes_t, weights_t)


def collect(blocks, *earlier):
    nb, h = len(blocks), blocks[0].shape[0]

    def body(*refs):
        for i in range(nb):
            refs[-1][i * h : (i + 1) * h, :] = refs[i][...]

    shape = jax.ShapeDtypeStruct((nb * h, blocks[0].shape[1]), BF)
    return on_chip(body, [*blocks, *earlier], [shape], 0, "collect")[0]


TOKEN = jax.ShapeDtypeStruct((8, 128), F32)


def forward(place, near, far, gate, up, down, T, e_total):
    E, D, F = gate.shape
    step = T + extra_rows(e_total, T, D)
    nb = near.shape[0] // step
    rows, wide, per = 2 * nb * T, E * F, e_total * T // D

    def body(place_ref, near_in, far_in, gate_ref, up_ref, down_ref, *refs):
        hid_refs, wa_refs, wb_refs = refs[0:2], refs[2:4], refs[4:6]
        hwt_ref, tokt_ref, near_ref, far_ref, token_ref, buf = refs[6:]
        token_ref[...] = jnp.zeros_like(token_ref)
        diagonal = lax.broadcasted_iota(jnp.int32, (T, T), 0) == lax.broadcasted_iota(
            jnp.int32, (T, T), 1
        )
        sublane = lax.broadcasted_iota(jnp.int32, (buf.shape[0], T), 0)
        buf[...] = jnp.zeros_like(buf)
        for side, source in enumerate((near_in, far_in)):
            for i in range(0, nb, 2):
                xs, ws = [], [[] for _ in range(E)]
                for b in (i, i + 1):
                    xs.append(source[b * step : b * step + T, :])
                    packed = source[b * step + T : (b + 1) * step, :].astype(F32)
                    buf[:per, :] = (
                        packed[:per] + packed[per : 2 * per] + packed[2 * per : 3 * per]
                    )
                    for j in range(E):
                        flat = (place_ref[2] * E + j) * T
                        at = pl.ds(pl.multiple_of(flat % D, T), T)
                        row = jnp.where(sublane == flat // D, buf[:, at], 0.0)
                        row = jnp.broadcast_to(jnp.sum(row, axis=0, keepdims=True), (T, T))
                        ws[j].append(
                            jnp.sum(jnp.where(diagonal, row, 0.0), axis=1, keepdims=True)
                        )
                x = jnp.concatenate(xs, axis=0)
                here = slice(i * T, (i + 2) * T)
                at = slice((side * nb + i) * T, (side * nb + i + 2) * T)
                tokt_ref[:, at] = x.T
                part = jnp.zeros((2 * T, D), F32)
                for j in range(E):
                    cols = slice(j * F, (j + 1) * F)
                    g = mm(x, gate_ref[j])
                    u = mm(x, up_ref[j])
                    w = jnp.concatenate(ws[j], axis=0)
                    s = jax.nn.sigmoid(g)
                    a = g * s
                    hid = a * u
                    hid_refs[side][here, cols] = hid.astype(BF)
                    wa_refs[side][here, cols] = (w * a).astype(BF)
                    wb_refs[side][here, cols] = (w * (u * s * (1.0 + g * (1.0 - s)))).astype(BF)
                    scaled = (w * hid).astype(BF)
                    hwt_ref[cols, at] = scaled.T
                    part = part + mm(scaled, down_ref[j])
                if side == 0:
                    near_ref[here, :] = part
                else:
                    far_ref[here, :] = part.astype(BF)

    out_shape = [jax.ShapeDtypeStruct((rows // 2, wide), BF)] * 6 + [
        jax.ShapeDtypeStruct((wide, rows), BF),
        jax.ShapeDtypeStruct((D, rows), BF),
        jax.ShapeDtypeStruct((rows // 2, D), F32),
        jax.ShapeDtypeStruct((rows // 2, D), BF),
        TOKEN,
    ]
    return on_chip(
        body,
        [place, near, far, gate, up, down],
        out_shape,
        6 * rows * D * wide,
        "forward",
        scalars=1,
        scratch=[pltpu.VMEM((-(-per // 8) * 8, D), F32)],
    )


def hidden_grads(cot, hid, wa, wb, down, *earlier):
    E, F, D = down.shape
    rows, wide = cot.shape[0], E * F
    step = 256

    def body(*refs):
        cot_ref, hid_ref, wa_ref, wb_ref, down_ref = refs[:5]
        gg_ref, ug_ref, rg_ref, token_ref = refs[5 + len(earlier) :]
        token_ref[...] = jnp.zeros_like(token_ref)
        lane = lax.broadcasted_iota(jnp.int32, (step, 128), 1)
        for m in range(0, rows, step):
            at = slice(m, m + step)
            c = cot_ref[at, :]
            total = jnp.zeros((step, 128), F32)
            for j in range(E):
                cols = slice(j * F, (j + 1) * F)
                h = mm_nt(c, down_ref[j])
                gg_ref[at, cols] = (h * wb_ref[at, cols].astype(F32)).astype(BF)
                ug_ref[at, cols] = (h * wa_ref[at, cols].astype(F32)).astype(BF)
                r = jnp.sum(h * hid_ref[at, cols].astype(F32), axis=1, keepdims=True)
                total = jnp.where(lane == j, r, total)
            rg_ref[at, :] = total

    out_shape = [jax.ShapeDtypeStruct((rows, wide), BF)] * 2 + [
        jax.ShapeDtypeStruct((rows, 128), F32),
        TOKEN,
    ]
    return on_chip(
        body,
        [cot, hid, wa, wb, down, *earlier],
        out_shape,
        2 * rows * D * wide,
        "hidden_grads",
    )


def token_partials(place, gg, ug, rg, gate, up, T, e_total, *earlier):
    half, wide = gg[0].shape
    E, D, F = gate.shape
    extra = extra_rows(e_total, T, D)
    step, nb, per = T + extra, half // T, e_total * T // D

    def body(*refs):
        place_ref = refs[0]
        gg_refs, ug_refs, rg_refs = refs[1:3], refs[3:5], refs[5:7]
        gate_ref, up_ref = refs[7:9]
        near_ref, far_ref, buf = refs[9 + len(earlier) :]
        sublane = lax.broadcasted_iota(jnp.int32, (extra, T), 0)
        for side in range(2):
            for i in range(0, nb, 2):
                at = slice(i * T, (i + 2) * T)
                part = jnp.zeros((2 * T, D), F32)
                for j in range(E):
                    cols = slice(j * F, (j + 1) * F)
                    part = part + mm_nt(gg_refs[side][at, cols], gate_ref[j])
                    part = part + mm_nt(ug_refs[side][at, cols], up_ref[j])
                for b in (i, i + 1):
                    buf[...] = jnp.zeros_like(buf)
                    turned = rg_refs[side][b * T : (b + 1) * T, :].T
                    for p, third in enumerate(thirds(turned[:8, :])):
                        for j in range(E):
                            flat = (place_ref[2] * E + j) * T
                            lanes = pl.ds(pl.multiple_of(flat % D, T), T)
                            mine = jnp.broadcast_to(third[j : j + 1, :], (extra, T))
                            row = sublane == p * per + flat // D
                            buf[:, lanes] = jnp.where(row, mine, buf[:, lanes])
                    mine = part[(b - i) * T : (b - i + 1) * T]
                    if side == 0:
                        near_ref[b * step : b * step + T, :] = mine
                        near_ref[b * step + T : (b + 1) * step, :] = buf[...]
                    else:
                        far_ref[b * step : b * step + T, :] = mine.astype(BF)
                        far_ref[b * step + T : (b + 1) * step, :] = buf[...].astype(BF)

    out_shape = [
        jax.ShapeDtypeStruct((nb * step, D), F32),
        jax.ShapeDtypeStruct((nb * step, D), BF),
    ]
    return on_chip(
        body,
        [place, *gg, *ug, *rg, gate, up, *earlier],
        out_shape,
        8 * half * D * wide,
        "token_partials",
        scalars=1,
        scratch=[pltpu.VMEM((extra, D), F32)],
    )


def weight_partials(place, lhs_t, rhs, experts, n, out_rows, name, *earlier):
    r = out_rows // (n * n)
    rows = lhs_t.shape[1]
    half = rows // 2
    joined = lhs_t.shape[0] != out_rows
    width = rhs[0].shape[1] // (1 if joined else experts)
    per = n * n if joined else 0

    def body(place_ref, left_ref, *refs):
        xi, yi = place_ref[0], place_ref[1]
        outs = refs[2 + len(earlier) : -1]
        refs[-1][...] = jnp.zeros_like(refs[-1])
        for k in [*range(1, n), 0]:
            for j in range(experts):
                left = []
                for q in range(n):
                    a, b = (k, q) if j % 2 == 0 else (q, k)
                    block = j * per + ((yi + b) % n) * n + (xi + a) % n
                    left.append(left_ref[pl.ds(pl.multiple_of(block * r, r), r), :])
                left = jnp.concatenate(left, axis=0)
                cols = slice(0, width) if joined else slice(j * width, (j + 1) * width)
                part = mm(left[:, :half], refs[0][:, cols]) + mm(left[:, half:], refs[1][:, cols])
                part = part.reshape(n, r, width)
                if k:
                    outs[2 * j][k - 1] = part.astype(BF)
                else:
                    outs[2 * j + 1][...] = part

    out_shape = [
        jax.ShapeDtypeStruct((n - 1, n, r, width), BF),
        jax.ShapeDtypeStruct((n, r, width), F32),
    ] * experts + [TOKEN]
    outs = on_chip(
        body,
        [place, lhs_t, *rhs, *earlier],
        out_shape,
        2 * experts * out_rows * width * rows,
        name,
        scalars=1,
    )
    return [(outs[2 * j], outs[2 * j + 1]) for j in range(experts)], outs[-1]


def add_first(parts, got, n, name, *earlier):
    E = len(parts)
    _, r, width = parts[0][1].shape

    def body(*refs):
        ins, outs = refs[: E * n], refs[E * n + len(earlier) :]
        outs[-1][...] = jnp.zeros_like(outs[-1])
        for j in range(E):
            for q in range(n):
                total = ins[j * n][q]
                for k in range(1, n):
                    total = total + ins[j * n + k][q].astype(F32)
                out = outs[j * n + q]
                out[...] = total.astype(out.dtype)

    operands = [v for j in range(E) for v in (parts[j][1], *got[j])]
    shapes = [jax.ShapeDtypeStruct((r, width), F32 if q == 0 else BF) for q in range(n)] * E
    outs = on_chip(body, [*operands, *earlier], shapes + [TOKEN], 0, name)
    return [outs[j * n : (j + 1) * n] for j in range(E)], outs[-1]


def collect_relayed(place, own, two, up, down, relayed, *earlier):
    h = own.shape[0]

    def body(place_ref, own_ref, two_ref, up_ref, down_ref, relayed_ref, *refs):
        out_ref = refs[-1]
        z = place_ref[2] // 2
        out_ref[:h, :] = own_ref[...]
        out_ref[2 * h : 3 * h, :] = two_ref[...]

        @pl.when(z == 0)
        def _():
            out_ref[h : 2 * h, :] = relayed_ref[...]

        @pl.when(z != 0)
        def _():
            out_ref[h : 2 * h, :] = up_ref[...]

        @pl.when(z == 3)
        def _():
            out_ref[3 * h :, :] = relayed_ref[...]

        @pl.when(z != 3)
        def _():
            out_ref[3 * h :, :] = down_ref[...]

    shape = jax.ShapeDtypeStruct((4 * h, own.shape[1]), BF)
    operands = [place, own, two, up, down, relayed, *earlier]
    return on_chip(body, operands, [shape], 0, "collect", scalars=1)[0]


def relay(totals, name, *earlier):
    sent = [v for total in totals for v in total[1:]]

    def body(*refs):
        outs = refs[len(sent) + len(earlier) :]
        outs[-1][...] = jnp.zeros_like(outs[-1])
        for source, out in zip(refs, outs[:-1]):
            out[...] = source[...]

    shapes = [jax.ShapeDtypeStruct(v.shape, v.dtype) for v in sent]
    *outs, done = on_chip(body, [*sent, *earlier], shapes + [TOKEN], 0, name)
    per = len(sent) // len(totals)
    return [[t[0], *outs[i * per : (i + 1) * per]] for i, t in enumerate(totals)], done


def add_second(totals, got, n, name, *earlier):
    E = len(totals)
    r, width = totals[0][0].shape

    def body(*refs):
        ins, (out_ref, token_ref) = refs[: E * n], refs[E * n + len(earlier) :]
        token_ref[...] = jnp.zeros_like(token_ref)
        for j in range(E):
            total = ins[j * n][...]
            for k in range(1, n):
                total = total + ins[j * n + k][...].astype(F32)
            out_ref[j] = total

    operands = [v for j in range(E) for v in (totals[j][0], *got[j])]
    return on_chip(
        body,
        [*operands, *earlier],
        [jax.ShapeDtypeStruct((E, r, width), F32), TOKEN],
        0,
        name,
    )


def add_sides(place, near, far, nz, name, *earlier):
    step, D = near.shape[0] // nz, near.shape[1]

    def body(place_ref, near_ref, far_ref, *refs):
        out_ref, token_ref = refs[len(earlier) :]
        token_ref[...] = jnp.zeros_like(token_ref)
        z = place_ref[2] // 2
        for k in range(nz):
            at = slice(k * step, (k + 1) * step)
            total = near_ref[at, :] + far_ref[at, :].astype(F32)
            to = pl.multiple_of((z - k + nz) % nz * step, step)
            out_ref[pl.ds(to, step), :] = total.astype(BF)

    shapes = [jax.ShapeDtypeStruct((nz * step, D), BF), TOKEN]
    return on_chip(body, [place, near, far, *earlier], shapes, 0, name, scalars=1)


def split_sides(near, far, nz, name, *earlier):
    step, D = near.shape[0] // nz, near.shape[1]

    def body(near_ref, far_ref, *refs):
        outs = refs[len(earlier) :]
        for k in range(nz):
            at = slice(k * step, (k + 1) * step)
            total = near_ref[at, :] + far_ref[at, :].astype(F32)
            outs[k][...] = total.astype(outs[k].dtype)

    shapes = [jax.ShapeDtypeStruct((step, D), F32 if k == 0 else BF) for k in range(nz)]
    return on_chip(body, [near, far, *earlier], shapes, 0, name)


def sum_rows(own, got, name, *earlier):
    def body(*refs):
        total = refs[0][...]
        for g in refs[1 : 1 + len(got)]:
            total = total + g[...].astype(F32)
        refs[-2][...] = total.astype(BF)
        refs[-1][...] = jnp.zeros_like(refs[-1])

    shapes = [jax.ShapeDtypeStruct(own.shape, BF), TOKEN]
    return on_chip(body, [own, *got, *earlier], shapes, 0, name)


def sum_rows_and_routes(got, routes_t, nz, e_total, name):
    top, T = routes_t.shape
    step, D = got.shape[0] // nz, got.shape[1]
    per, lanes = e_total * T // D, D // T

    def body(*refs):
        routes_ref, got_ref, rows_ref, routes_out, token_ref = refs
        token_ref[...] = jnp.zeros_like(token_ref)
        total = got_ref[:step, :].astype(F32)
        for k in range(1, nz):
            total = total + got_ref[k * step : (k + 1) * step, :].astype(F32)
        rows_ref[...] = total[:T].astype(BF)
        packed = total[T:]
        packed = packed[:per] + packed[per : 2 * per] + packed[2 * per : 3 * per]
        grads = jnp.zeros((top, T), F32)
        for i in range(e_total):
            at = slice(i % lanes * T, (i % lanes + 1) * T)
            row = packed[i // lanes : i // lanes + 1, at]
            grads = jnp.where(routes_ref[...] == i, row, grads)
        routes_out[...] = grads

    shapes = [
        jax.ShapeDtypeStruct((T, D), BF),
        jax.ShapeDtypeStruct((top, T), F32),
        TOKEN,
    ]
    return on_chip(body, [routes_t, got], shapes, 0, name)


def local(tokens, routes, route_weights, gate_weight, up_weight, down_weight, cotangent):
    dp = lax.axis_size("dp")
    ne = lax.axis_size("expert")
    n = math.isqrt(dp)
    nz = ne // 2
    T, D = tokens.shape
    E, _, F = gate_weight.shape
    e_total = E * ne
    d = lax.axis_index("dp")
    e = lax.axis_index("expert")
    place = jnp.stack([d % n, d // n, e]).astype(jnp.int32)

    def swap(v):
        return lax.ppermute(v, "expert", [(i, i ^ 1) for i in range(ne)])

    def move_z(v, k):
        pairs = [(2 * z + c, 2 * ((z + k) % nz) + c) for z in range(nz) for c in range(2)]
        return lax.ppermute(v, "expert", pairs)

    def move_x(v, k):
        pairs = [(y * n + x, y * n + (x + k) % n) for y in range(n) for x in range(n)]
        return lax.ppermute(v, "dp", pairs)

    def move_y(v, k):
        pairs = [(y * n + x, ((y + k) % n) * n + x) for y in range(n) for x in range(n)]
        return lax.ppermute(v, "dp", pairs)

    def gather_near(v):
        return [v] + [move_z(v, k) for k in range(1, nz)]

    def chip_pairs(pairs):
        return [(2 * a + c, 2 * b + c) for a, b in pairs for c in range(2)]

    def near_rows(v, *earlier):
        if nz != 4:
            return collect(gather_near(v), *earlier)
        send = lambda u, pairs: lax.ppermute(u, "expert", chip_pairs(pairs))
        two = move_z(v, 2)
        up = send(v, [(0, 1), (1, 2), (2, 3)])
        down = send(v, [(1, 0), (2, 1), (3, 2)])
        relayed = send(two, [(2, 3), (1, 0)])
        return collect_relayed(place, v, two, up, down, relayed, *earlier)

    packed = pack_tokens(tokens, routes.T, route_weights.T, e_total)
    token_near = near_rows(packed)
    cot_blocks = gather_near(cotangent)
    token_far = swap(token_near)
    *saved, hw_t, tok_t, out_near, out_far, forward_done = forward(
        place, token_near, token_far, gate_weight, up_weight, down_weight, T, e_total
    )
    hid, wa, wb = saved[0:2], saved[2:4], saved[4:6]
    out_far = swap(out_far)
    cot_near = collect(cot_blocks, forward_done)
    cot_far = swap(cot_near)

    def send_first(parts):
        got = []
        for j, (sent, _) in enumerate(parts):
            move = move_x if j % 2 == 0 else move_y
            got.append([move(sent[k - 1], k) for k in range(1, n)])
        return got

    def send_second(totals):
        got = []
        for j, total in enumerate(totals):
            move = move_y if j % 2 == 0 else move_x
            got.append([move(total[k], k) for k in range(1, n)])
        return got

    z_groups = [[2 * z + c for z in range(nz)] for c in range(2)]

    def send_home(parts):
        return lax.all_to_all(
            parts,
            "expert",
            split_axis=0,
            concat_axis=0,
            tiled=True,
            axis_index_groups=z_groups,
        )

    gg0, ug0, rg0, near_done = hidden_grads(cot_near, hid[0], wa[0], wb[0], down_weight)
    down_part, down_done = weight_partials(
        place, hw_t, [cot_near, cot_far], E, n, F, "down_partials", near_done
    )
    down_got = send_first(down_part)
    gg1, ug1, rg1, _ = hidden_grads(cot_far, hid[1], wa[1], wb[1], down_weight, down_done)
    gate_part, gate_done = weight_partials(place, tok_t, [gg0, gg1], E, n, D, "gate_partials")
    gate_got = send_first(gate_part)
    out_parts = split_sides(out_near, out_far, nz, "out_sides", down_done)
    out_got = [move_z(out_parts[k], -k) for k in range(1, nz)]
    down_totals, down_mid = add_first(down_part, down_got, n, "down_first", gate_done, out_got[0])
    tg_near, tg_far = token_partials(
        place,
        [gg0, gg1],
        [ug0, ug1],
        [rg0, rg1],
        gate_weight,
        up_weight,
        T,
        e_total,
        down_mid,
    )
    tg_far = swap(tg_far)
    up_part, up_done = weight_partials(
        place, tok_t, [ug0, ug1], E, n, D, "up_partials", tg_near[:8, :128]
    )
    up_got = send_first(up_part)
    layer_out, out_done = sum_rows(out_parts[0], out_got, "out_rows", up_done)
    tg_parts, tg_done = add_sides(place, tg_near, tg_far, nz, "token_sides", out_done)
    tg_got = send_home(tg_parts)
    down_totals, down_mid = relay(down_totals, "down_relay", tg_done)
    down_got = send_second(down_totals)
    gate_totals, gate_mid = add_first(gate_part, gate_got, n, "gate_first", down_mid)
    gate_got = send_second(gate_totals)
    up_totals, up_mid = add_first(up_part, up_got, n, "up_first", gate_mid)
    up_got = send_second(up_totals)
    down_grads, down_done = add_second(down_totals, down_got, n, "down_second", up_mid)
    gate_grads, gate_done = add_second(gate_totals, gate_got, n, "gate_second", down_done)
    token_grads, route_grads_t, rows_done = sum_rows_and_routes(
        tg_got, routes.T, nz, e_total, "token_rows"
    )
    up_grads, _ = add_second(up_totals, up_got, n, "up_second", gate_done, rows_done)
    route_grads = route_grads_t.T

    return (layer_out, token_grads, route_grads, gate_grads, up_grads, down_grads)


def solution(mesh):
    rows = P(("dp", "expert"), None)
    weight = P("expert", None, None)
    grad = P("expert", "dp", None)
    return jax.shard_map(
        local,
        mesh=mesh,
        in_specs=(rows, rows, rows, weight, weight, weight, rows),
        out_specs=(rows, rows, rows, grad, grad, grad),
        check_vma=False,
    )
```

```python
import math

import jax
import jax.numpy as jnp
from jax import lax
from jax.experimental import pallas as pl
from jax.experimental.pallas import tpu as pltpu
from jax.sharding import PartitionSpec as P

BF = jnp.bfloat16
F32 = jnp.float32
VMEM = pl.BlockSpec(memory_space=pltpu.VMEM)
SMEM = pl.BlockSpec(memory_space=pltpu.SMEM)
NT = (((1,), (1,)), ((), ()))


def mm(a, b):
    return jnp.dot(a, b, preferred_element_type=F32)


def mm_nt(a, b):
    return lax.dot_general(a, b, NT, preferred_element_type=F32)


def size(s):
    return math.prod(s.shape) * jnp.dtype(s.dtype).itemsize


def on_chip(body, operands, out_shape, flops, name, scalars=0, scratch=()):
    total = sum(size(s) for s in list(operands) + list(out_shape))
    limit = min(60 * 2**20, total // 8 + sum(size(s) for s in scratch) + 4 * 2**20)
    return pl.pallas_call(
        body,
        in_specs=[SMEM] * scalars + [VMEM] * (len(operands) - scalars),
        out_specs=[VMEM] * len(out_shape),
        out_shape=out_shape,
        scratch_shapes=list(scratch),
        compiler_params=pltpu.CompilerParams(vmem_limit_bytes=limit),
        cost_estimate=pl.CostEstimate(
            flops=10**10, bytes_accessed=total, transcendentals=0
        ),
        name=name,
    )(*operands)


def extra_rows(e_total, T, D):
    return -(-3 * e_total * T // (8 * D)) * 8


def thirds(v):
    hi = v.astype(BF).astype(F32)
    mid = (v - hi).astype(BF).astype(F32)
    return hi, mid, v - hi - mid


def pack_tokens(tokens, routes_t, weights_t, e_total):
    T, D = tokens.shape
    extra = extra_rows(e_total, T, D)
    per = D // T

    def body(tok_hbm, routes_hbm, weights_hbm, out_ref, routes_ref, weights_ref, buf, sems):
        copies = [
            pltpu.make_async_copy(routes_hbm, routes_ref, sems.at[0]),
            pltpu.make_async_copy(weights_hbm, weights_ref, sems.at[1]),
            pltpu.make_async_copy(tok_hbm, out_ref.at[pl.ds(0, T)], sems.at[2]),
        ]
        for c in copies:
            c.start()
        buf[...] = jnp.zeros_like(buf)
        expert = lax.broadcasted_iota(jnp.int32, (e_total, T), 0)
        dense = jnp.zeros((e_total, T), F32)
        copies[0].wait()
        copies[1].wait()
        for k in range(routes_t.shape[0]):
            dense = dense + jnp.where(
                routes_ref[k : k + 1, :] == expert, weights_ref[k : k + 1, :], 0.0
            )
        for p, part in enumerate(thirds(dense)):
            for i in range(e_total):
                row = p * (e_total // per) + i // per
                at = slice(i % per * T, (i % per + 1) * T)
                buf[row : row + 1, at] = part[i : i + 1, :]
        out_ref[T:, :] = buf[...].astype(BF)
        copies[2].wait()

    return pl.pallas_call(
        body,
        in_specs=[pl.BlockSpec(memory_space=pl.ANY)] * 3,
        out_specs=VMEM,
        out_shape=jax.ShapeDtypeStruct((T + extra, D), BF),
        scratch_shapes=[
            pltpu.VMEM(routes_t.shape, jnp.int32),
            pltpu.VMEM(weights_t.shape, F32),
            pltpu.VMEM((extra, D), F32),
            pltpu.SemaphoreType.DMA((3,)),
        ],
        compiler_params=pltpu.CompilerParams(vmem_limit_bytes=60 * 2**20),
        cost_estimate=pl.CostEstimate(flops=10**10, bytes_accessed=2**20, transcendentals=0),
        name="pack_tokens",
    )(tokens, routes_t, weights_t)


def collect(blocks, *earlier):
    nb, h = len(blocks), blocks[0].shape[0]

    def body(*refs):
        for i in range(nb):
            refs[-1][i * h : (i + 1) * h, :] = refs[i][...]

    shape = jax.ShapeDtypeStruct((nb * h, blocks[0].shape[1]), BF)
    return on_chip(body, [*blocks, *earlier], [shape], 0, "collect")[0]


TOKEN = jax.ShapeDtypeStruct((8, 128), F32)


def forward(place, near, far, gate, up, down, T, e_total):
    E, D, F = gate.shape
    step = T + extra_rows(e_total, T, D)
    nb = near.shape[0] // step
    rows, wide, per = 2 * nb * T, E * F, e_total * T // D

    def body(place_ref, near_in, far_in, gate_ref, up_ref, down_ref, *refs):
        hid_refs, wa_refs, wb_refs = refs[0:2], refs[2:4], refs[4:6]
        hwt_ref, tokt_ref, near_ref, far_ref, token_ref, buf = refs[6:]
        token_ref[...] = jnp.zeros_like(token_ref)
        diagonal = lax.broadcasted_iota(jnp.int32, (T, T), 0) == lax.broadcasted_iota(
            jnp.int32, (T, T), 1
        )
        sublane = lax.broadcasted_iota(jnp.int32, (buf.shape[0], T), 0)
        buf[...] = jnp.zeros_like(buf)
        for side, source in enumerate((near_in, far_in)):
            for i in range(0, nb, 2):
                xs, ws = [], [[] for _ in range(E)]
                for b in (i, i + 1):
                    xs.append(source[b * step : b * step + T, :])
                    packed = source[b * step + T : (b + 1) * step, :].astype(F32)
                    buf[:per, :] = (
                        packed[:per] + packed[per : 2 * per] + packed[2 * per : 3 * per]
                    )
                    for j in range(E):
                        flat = (place_ref[2] * E + j) * T
                        at = pl.ds(pl.multiple_of(flat % D, T), T)
                        row = jnp.where(sublane == flat // D, buf[:, at], 0.0)
                        row = jnp.broadcast_to(jnp.sum(row, axis=0, keepdims=True), (T, T))
                        ws[j].append(
                            jnp.sum(jnp.where(diagonal, row, 0.0), axis=1, keepdims=True)
                        )
                x = jnp.concatenate(xs, axis=0)
                here = slice(i * T, (i + 2) * T)
                at = slice((side * nb + i) * T, (side * nb + i + 2) * T)
                tokt_ref[:, at] = x.T
                part = jnp.zeros((2 * T, D), F32)
                for j in range(E):
                    cols = slice(j * F, (j + 1) * F)
                    g = mm(x, gate_ref[j])
                    u = mm(x, up_ref[j])
                    w = jnp.concatenate(ws[j], axis=0)
                    s = jax.nn.sigmoid(g)
                    a = g * s
                    hid = a * u
                    hid_refs[side][here, cols] = hid.astype(BF)
                    wa_refs[side][here, cols] = (w * a).astype(BF)
                    wb_refs[side][here, cols] = (w * (u * s * (1.0 + g * (1.0 - s)))).astype(BF)
                    scaled = (w * hid).astype(BF)
                    hwt_ref[cols, at] = scaled.T
                    part = part + mm(scaled, down_ref[j])
                if side == 0:
                    near_ref[here, :] = part
                else:
                    far_ref[here, :] = part.astype(BF)

    out_shape = [jax.ShapeDtypeStruct((rows // 2, wide), BF)] * 6 + [
        jax.ShapeDtypeStruct((wide, rows), BF),
        jax.ShapeDtypeStruct((D, rows), BF),
        jax.ShapeDtypeStruct((rows // 2, D), F32),
        jax.ShapeDtypeStruct((rows // 2, D), BF),
        TOKEN,
    ]
    return on_chip(
        body,
        [place, near, far, gate, up, down],
        out_shape,
        6 * rows * D * wide,
        "forward",
        scalars=1,
        scratch=[pltpu.VMEM((-(-per // 8) * 8, D), F32)],
    )


def hidden_grads(cot, hid, wa, wb, down, *earlier):
    E, F, D = down.shape
    rows, wide = cot.shape[0], E * F
    step = 256

    def body(*refs):
        cot_ref, hid_ref, wa_ref, wb_ref, down_ref = refs[:5]
        gg_ref, ug_ref, rg_ref, token_ref = refs[5 + len(earlier) :]
        token_ref[...] = jnp.zeros_like(token_ref)
        lane = lax.broadcasted_iota(jnp.int32, (step, 128), 1)
        for m in range(0, rows, step):
            at = slice(m, m + step)
            c = cot_ref[at, :]
            total = jnp.zeros((step, 128), F32)
            for j in range(E):
                cols = slice(j * F, (j + 1) * F)
                h = mm_nt(c, down_ref[j])
                gg_ref[at, cols] = (h * wb_ref[at, cols].astype(F32)).astype(BF)
                ug_ref[at, cols] = (h * wa_ref[at, cols].astype(F32)).astype(BF)
                r = jnp.sum(h * hid_ref[at, cols].astype(F32), axis=1, keepdims=True)
                total = jnp.where(lane == j, r, total)
            rg_ref[at, :] = total

    out_shape = [jax.ShapeDtypeStruct((rows, wide), BF)] * 2 + [
        jax.ShapeDtypeStruct((rows, 128), F32),
        TOKEN,
    ]
    return on_chip(
        body,
        [cot, hid, wa, wb, down, *earlier],
        out_shape,
        2 * rows * D * wide,
        "hidden_grads",
    )


def token_partials(place, gg, ug, rg, gate, up, T, e_total, *earlier):
    half, wide = gg[0].shape
    E, D, F = gate.shape
    extra = extra_rows(e_total, T, D)
    step, nb, per = T + extra, half // T, e_total * T // D

    def body(*refs):
        place_ref = refs[0]
        gg_refs, ug_refs, rg_refs = refs[1:3], refs[3:5], refs[5:7]
        gate_ref, up_ref = refs[7:9]
        near_ref, far_ref, buf = refs[9 + len(earlier) :]
        sublane = lax.broadcasted_iota(jnp.int32, (extra, T), 0)
        for side in range(2):
            for i in range(0, nb, 2):
                at = slice(i * T, (i + 2) * T)
                part = jnp.zeros((2 * T, D), F32)
                for j in range(E):
                    cols = slice(j * F, (j + 1) * F)
                    part = part + mm_nt(gg_refs[side][at, cols], gate_ref[j])
                    part = part + mm_nt(ug_refs[side][at, cols], up_ref[j])
                for b in (i, i + 1):
                    buf[...] = jnp.zeros_like(buf)
                    turned = rg_refs[side][b * T : (b + 1) * T, :].T
                    for p, third in enumerate(thirds(turned[:8, :])):
                        for j in range(E):
                            flat = (place_ref[2] * E + j) * T
                            lanes = pl.ds(pl.multiple_of(flat % D, T), T)
                            mine = jnp.broadcast_to(third[j : j + 1, :], (extra, T))
                            row = sublane == p * per + flat // D
                            buf[:, lanes] = jnp.where(row, mine, buf[:, lanes])
                    mine = part[(b - i) * T : (b - i + 1) * T]
                    if side == 0:
                        near_ref[b * step : b * step + T, :] = mine
                        near_ref[b * step + T : (b + 1) * step, :] = buf[...]
                    else:
                        far_ref[b * step : b * step + T, :] = mine.astype(BF)
                        far_ref[b * step + T : (b + 1) * step, :] = buf[...].astype(BF)

    out_shape = [
        jax.ShapeDtypeStruct((nb * step, D), F32),
        jax.ShapeDtypeStruct((nb * step, D), BF),
    ]
    return on_chip(
        body,
        [place, *gg, *ug, *rg, gate, up, *earlier],
        out_shape,
        8 * half * D * wide,
        "token_partials",
        scalars=1,
        scratch=[pltpu.VMEM((extra, D), F32)],
    )


def weight_partials(place, lhs_t, rhs, experts, n, out_rows, name, *earlier):
    r = out_rows // (n * n)
    rows = lhs_t.shape[1]
    half = rows // 2
    joined = lhs_t.shape[0] != out_rows
    width = rhs[0].shape[1] // (1 if joined else experts)
    per = n * n if joined else 0

    def body(place_ref, left_ref, *refs):
        xi, yi = place_ref[0], place_ref[1]
        outs = refs[2 + len(earlier) : -1]
        refs[-1][...] = jnp.zeros_like(refs[-1])
        for k in [*range(1, n), 0]:
            for j in range(experts):
                left = []
                for q in range(n):
                    a, b = (k, q) if j % 2 == 0 else (q, k)
                    block = j * per + ((yi + b) % n) * n + (xi + a) % n
                    left.append(left_ref[pl.ds(pl.multiple_of(block * r, r), r), :])
                left = jnp.concatenate(left, axis=0)
                cols = slice(0, width) if joined else slice(j * width, (j + 1) * width)
                part = mm(left[:, :half], refs[0][:, cols]) + mm(left[:, half:], refs[1][:, cols])
                part = part.reshape(n, r, width)
                if k:
                    outs[2 * j][k - 1] = part.astype(BF)
                else:
                    outs[2 * j + 1][...] = part

    out_shape = [
        jax.ShapeDtypeStruct((n - 1, n, r, width), BF),
        jax.ShapeDtypeStruct((n, r, width), F32),
    ] * experts + [TOKEN]
    outs = on_chip(
        body,
        [place, lhs_t, *rhs, *earlier],
        out_shape,
        2 * experts * out_rows * width * rows,
        name,
        scalars=1,
    )
    return [(outs[2 * j], outs[2 * j + 1]) for j in range(experts)], outs[-1]


def add_first(parts, got, n, name, *earlier):
    E = len(parts)
    _, r, width = parts[0][1].shape

    def body(*refs):
        ins, outs = refs[: E * n], refs[E * n + len(earlier) :]
        outs[-1][...] = jnp.zeros_like(outs[-1])
        for j in range(E):
            for q in range(n):
                total = ins[j * n][q]
                for k in range(1, n):
                    total = total + ins[j * n + k][q].astype(F32)
                out = outs[j * n + q]
                out[...] = total.astype(out.dtype)

    operands = [v for j in range(E) for v in (parts[j][1], *got[j])]
    shapes = [jax.ShapeDtypeStruct((r, width), F32 if q == 0 else BF) for q in range(n)] * E
    outs = on_chip(body, [*operands, *earlier], shapes + [TOKEN], 0, name)
    return [outs[j * n : (j + 1) * n] for j in range(E)], outs[-1]


def collect_relayed(place, own, two, up, down, relayed, *earlier):
    h = own.shape[0]

    def body(place_ref, own_ref, two_ref, up_ref, down_ref, relayed_ref, *refs):
        out_ref = refs[-1]
        z = place_ref[2] // 2
        out_ref[:h, :] = own_ref[...]
        out_ref[2 * h : 3 * h, :] = two_ref[...]

        @pl.when(z == 0)
        def _():
            out_ref[h : 2 * h, :] = relayed_ref[...]

        @pl.when(z != 0)
        def _():
            out_ref[h : 2 * h, :] = up_ref[...]

        @pl.when(z == 3)
        def _():
            out_ref[3 * h :, :] = relayed_ref[...]

        @pl.when(z != 3)
        def _():
            out_ref[3 * h :, :] = down_ref[...]

    shape = jax.ShapeDtypeStruct((4 * h, own.shape[1]), BF)
    operands = [place, own, two, up, down, relayed, *earlier]
    return on_chip(body, operands, [shape], 0, "collect", scalars=1)[0]


def relay(totals, name, *earlier):
    sent = [v for total in totals for v in total[1:]]

    def body(*refs):
        outs = refs[len(sent) + len(earlier) :]
        outs[-1][...] = jnp.zeros_like(outs[-1])
        for source, out in zip(refs, outs[:-1]):
            out[...] = source[...]

    shapes = [jax.ShapeDtypeStruct(v.shape, v.dtype) for v in sent]
    *outs, done = on_chip(body, [*sent, *earlier], shapes + [TOKEN], 0, name)
    per = len(sent) // len(totals)
    return [[t[0], *outs[i * per : (i + 1) * per]] for i, t in enumerate(totals)], done


def add_second(totals, got, n, name, *earlier):
    E = len(totals)
    r, width = totals[0][0].shape

    def body(*refs):
        ins, (out_ref, token_ref) = refs[: E * n], refs[E * n + len(earlier) :]
        token_ref[...] = jnp.zeros_like(token_ref)
        for j in range(E):
            total = ins[j * n][...]
            for k in range(1, n):
                total = total + ins[j * n + k][...].astype(F32)
            out_ref[j] = total

    operands = [v for j in range(E) for v in (totals[j][0], *got[j])]
    return on_chip(
        body,
        [*operands, *earlier],
        [jax.ShapeDtypeStruct((E, r, width), F32), TOKEN],
        0,
        name,
    )


def add_sides(place, near, far, nz, name, *earlier):
    step, D = near.shape[0] // nz, near.shape[1]

    def body(place_ref, near_ref, far_ref, *refs):
        out_ref, token_ref = refs[len(earlier) :]
        token_ref[...] = jnp.zeros_like(token_ref)
        z = place_ref[2] // 2
        for k in range(nz):
            at = slice(k * step, (k + 1) * step)
            total = near_ref[at, :] + far_ref[at, :].astype(F32)
            to = pl.multiple_of((z - k + nz) % nz * step, step)
            out_ref[pl.ds(to, step), :] = total.astype(BF)

    shapes = [jax.ShapeDtypeStruct((nz * step, D), BF), TOKEN]
    return on_chip(body, [place, near, far, *earlier], shapes, 0, name, scalars=1)


def split_sides(near, far, nz, name, *earlier):
    step, D = near.shape[0] // nz, near.shape[1]

    def body(near_ref, far_ref, *refs):
        outs = refs[len(earlier) :]
        for k in range(nz):
            at = slice(k * step, (k + 1) * step)
            total = near_ref[at, :] + far_ref[at, :].astype(F32)
            outs[k][...] = total.astype(outs[k].dtype)

    shapes = [jax.ShapeDtypeStruct((step, D), F32 if k == 0 else BF) for k in range(nz)]
    return on_chip(body, [near, far, *earlier], shapes, 0, name)


def sum_rows(own, got, name, *earlier):
    def body(*refs):
        total = refs[0][...]
        for g in refs[1 : 1 + len(got)]:
            total = total + g[...].astype(F32)
        refs[-2][...] = total.astype(BF)
        refs[-1][...] = jnp.zeros_like(refs[-1])

    shapes = [jax.ShapeDtypeStruct(own.shape, BF), TOKEN]
    return on_chip(body, [own, *got, *earlier], shapes, 0, name)


def sum_rows_and_routes(got, routes_t, nz, e_total, name):
    top, T = routes_t.shape
    step, D = got.shape[0] // nz, got.shape[1]
    per, lanes = e_total * T // D, D // T

    def body(*refs):
        routes_ref, got_ref, rows_ref, routes_out, token_ref = refs
        token_ref[...] = jnp.zeros_like(token_ref)
        total = got_ref[:step, :].astype(F32)
        for k in range(1, nz):
            total = total + got_ref[k * step : (k + 1) * step, :].astype(F32)
        rows_ref[...] = total[:T].astype(BF)
        packed = total[T:]
        packed = packed[:per] + packed[per : 2 * per] + packed[2 * per : 3 * per]
        grads = jnp.zeros((top, T), F32)
        for i in range(e_total):
            at = slice(i % lanes * T, (i % lanes + 1) * T)
            row = packed[i // lanes : i // lanes + 1, at]
            grads = jnp.where(routes_ref[...] == i, row, grads)
        routes_out[...] = grads

    shapes = [
        jax.ShapeDtypeStruct((T, D), BF),
        jax.ShapeDtypeStruct((top, T), F32),
        TOKEN,
    ]
    return on_chip(body, [routes_t, got], shapes, 0, name)


def local(tokens, routes, route_weights, gate_weight, up_weight, down_weight, cotangent):
    dp = lax.axis_size("dp")
    ne = lax.axis_size("expert")
    n = math.isqrt(dp)
    nz = ne // 2
    T, D = tokens.shape
    E, _, F = gate_weight.shape
    e_total = E * ne
    d = lax.axis_index("dp")
    e = lax.axis_index("expert")
    place = jnp.stack([d % n, d // n, e]).astype(jnp.int32)

    def swap(v):
        return lax.ppermute(v, "expert", [(i, i ^ 1) for i in range(ne)])

    def move_z(v, k):
        pairs = [(2 * z + c, 2 * ((z + k) % nz) + c) for z in range(nz) for c in range(2)]
        return lax.ppermute(v, "expert", pairs)

    def move_x(v, k):
        pairs = [(y * n + x, y * n + (x + k) % n) for y in range(n) for x in range(n)]
        return lax.ppermute(v, "dp", pairs)

    def move_y(v, k):
        pairs = [(y * n + x, ((y + k) % n) * n + x) for y in range(n) for x in range(n)]
        return lax.ppermute(v, "dp", pairs)

    def gather_near(v):
        return [v] + [move_z(v, k) for k in range(1, nz)]

    def chip_pairs(pairs):
        return [(2 * a + c, 2 * b + c) for a, b in pairs for c in range(2)]

    def near_rows(v, *earlier):
        if nz != 4:
            return collect(gather_near(v), *earlier)
        send = lambda u, pairs: lax.ppermute(u, "expert", chip_pairs(pairs))
        two = move_z(v, 2)
        up = send(v, [(0, 1), (1, 2), (2, 3)])
        down = send(v, [(1, 0), (2, 1), (3, 2)])
        relayed = send(two, [(2, 3), (1, 0)])
        return collect_relayed(place, v, two, up, down, relayed, *earlier)

    packed = pack_tokens(tokens, routes.T, route_weights.T, e_total)
    token_near = near_rows(packed)
    cot_blocks = gather_near(cotangent)
    token_far = swap(token_near)
    *saved, hw_t, tok_t, out_near, out_far, forward_done = forward(
        place, token_near, token_far, gate_weight, up_weight, down_weight, T, e_total
    )
    hid, wa, wb = saved[0:2], saved[2:4], saved[4:6]
    out_far = swap(out_far)
    cot_near = collect(cot_blocks, forward_done)
    cot_far = swap(cot_near)

    def send_first(parts):
        got = []
        for j, (sent, _) in enumerate(parts):
            move = move_x if j % 2 == 0 else move_y
            got.append([move(sent[k - 1], k) for k in range(1, n)])
        return got

    def send_second(totals):
        got = []
        for j, total in enumerate(totals):
            move = move_y if j % 2 == 0 else move_x
            got.append([move(total[k], k) for k in range(1, n)])
        return got

    z_groups = [[2 * z + c for z in range(nz)] for c in range(2)]

    def send_home(parts):
        return lax.all_to_all(
            parts,
            "expert",
            split_axis=0,
            concat_axis=0,
            tiled=True,
            axis_index_groups=z_groups,
        )

    gg0, ug0, rg0, near_done = hidden_grads(cot_near, hid[0], wa[0], wb[0], down_weight)
    down_part, down_done = weight_partials(
        place, hw_t, [cot_near, cot_far], E, n, F, "down_partials", near_done
    )
    down_got = send_first(down_part)
    gg1, ug1, rg1, _ = hidden_grads(cot_far, hid[1], wa[1], wb[1], down_weight, down_done)
    gate_part, gate_done = weight_partials(place, tok_t, [gg0, gg1], E, n, D, "gate_partials")
    gate_got = send_first(gate_part)
    out_parts = split_sides(out_near, out_far, nz, "out_sides", down_done)
    out_got = [move_z(out_parts[k], -k) for k in range(1, nz)]
    down_totals, down_mid = add_first(down_part, down_got, n, "down_first", gate_done, out_got[0])
    tg_near, tg_far = token_partials(
        place,
        [gg0, gg1],
        [ug0, ug1],
        [rg0, rg1],
        gate_weight,
        up_weight,
        T,
        e_total,
        down_mid,
    )
    tg_far = swap(tg_far)
    up_part, up_done = weight_partials(
        place, tok_t, [ug0, ug1], E, n, D, "up_partials", tg_near[:8, :128]
    )
    up_got = send_first(up_part)
    layer_out, out_done = sum_rows(out_parts[0], out_got, "out_rows", up_done)
    tg_parts, tg_done = add_sides(place, tg_near, tg_far, nz, "token_sides", out_done)
    tg_got = send_home(tg_parts)
    down_totals, down_mid = relay(down_totals, "down_relay", tg_done)
    down_got = send_second(down_totals)
    gate_totals, gate_mid = add_first(gate_part, gate_got, n, "gate_first", down_mid)
    gate_got = send_second(gate_totals)
    up_totals, up_mid = add_first(up_part, up_got, n, "up_first", gate_mid)
    up_got = send_second(up_totals)
    down_grads, down_done = add_second(down_totals, down_got, n, "down_second", up_mid)
    gate_grads, gate_done = add_second(gate_totals, gate_got, n, "gate_second", down_done)
    token_grads, route_grads_t, rows_done = sum_rows_and_routes(
        tg_got, routes.T, nz, e_total, "token_rows"
    )
    up_grads, _ = add_second(up_totals, up_got, n, "up_second", gate_done, rows_done)
    route_grads = route_grads_t.T

    return (layer_out, token_grads, route_grads, gate_grads, up_grads, down_grads)


def solution(mesh):
    rows = P(("dp", "expert"), None)
    weight = P("expert", None, None)
    grad = P("expert", "dp", None)
    return jax.shard_map(
        local,
        mesh=mesh,
        in_specs=(rows, rows, rows, weight, weight, weight, rows),
        out_specs=(rows, rows, rows, grad, grad, grad),
        check_vma=False,
    )
```

```python
import math

import jax
import jax.numpy as jnp
from jax import lax
from jax.experimental import pallas as pl
from jax.experimental.pallas import tpu as pltpu
from jax.sharding import PartitionSpec as P

BF = jnp.bfloat16
F32 = jnp.float32
VMEM = pl.BlockSpec(memory_space=pltpu.VMEM)
SMEM = pl.BlockSpec(memory_space=pltpu.SMEM)
NT = (((1,), (1,)), ((), ()))


def mm(a, b):
    return jnp.dot(a, b, preferred_element_type=F32)


def mm_nt(a, b):
    return lax.dot_general(a, b, NT, preferred_element_type=F32)


def size(s):
    return math.prod(s.shape) * jnp.dtype(s.dtype).itemsize


def on_chip(body, operands, out_shape, flops, name, scalars=0, scratch=()):
    total = sum(size(s) for s in list(operands) + list(out_shape))
    limit = min(60 * 2**20, total // 8 + sum(size(s) for s in scratch) + 4 * 2**20)
    return pl.pallas_call(
        body,
        in_specs=[SMEM] * scalars + [VMEM] * (len(operands) - scalars),
        out_specs=[VMEM] * len(out_shape),
        out_shape=out_shape,
        scratch_shapes=list(scratch),
        compiler_params=pltpu.CompilerParams(vmem_limit_bytes=limit),
        cost_estimate=pl.CostEstimate(
            flops=10**10, bytes_accessed=total, transcendentals=0
        ),
        name=name,
    )(*operands)


def extra_rows(e_total, T, D):
    return -(-3 * e_total * T // (8 * D)) * 8


def thirds(v):
    hi = v.astype(BF).astype(F32)
    mid = (v - hi).astype(BF).astype(F32)
    return hi, mid, v - hi - mid


def pack_tokens(tokens, routes_t, weights_t, e_total):
    T, D = tokens.shape
    extra = extra_rows(e_total, T, D)
    per = D // T

    def body(tok_hbm, routes_hbm, weights_hbm, out_ref, routes_ref, weights_ref, buf, sems):
        copies = [
            pltpu.make_async_copy(routes_hbm, routes_ref, sems.at[0]),
            pltpu.make_async_copy(weights_hbm, weights_ref, sems.at[1]),
            pltpu.make_async_copy(tok_hbm, out_ref.at[pl.ds(0, T)], sems.at[2]),
        ]
        for c in copies:
            c.start()
        buf[...] = jnp.zeros_like(buf)
        expert = lax.broadcasted_iota(jnp.int32, (e_total, T), 0)
        dense = jnp.zeros((e_total, T), F32)
        copies[0].wait()
        copies[1].wait()
        for k in range(routes_t.shape[0]):
            dense = dense + jnp.where(
                routes_ref[k : k + 1, :] == expert, weights_ref[k : k + 1, :], 0.0
            )
        for p, part in enumerate(thirds(dense)):
            for i in range(e_total):
                row = p * (e_total // per) + i // per
                at = slice(i % per * T, (i % per + 1) * T)
                buf[row : row + 1, at] = part[i : i + 1, :]
        out_ref[T:, :] = buf[...].astype(BF)
        copies[2].wait()

    return pl.pallas_call(
        body,
        in_specs=[pl.BlockSpec(memory_space=pl.ANY)] * 3,
        out_specs=VMEM,
        out_shape=jax.ShapeDtypeStruct((T + extra, D), BF),
        scratch_shapes=[
            pltpu.VMEM(routes_t.shape, jnp.int32),
            pltpu.VMEM(weights_t.shape, F32),
            pltpu.VMEM((extra, D), F32),
            pltpu.SemaphoreType.DMA((3,)),
        ],
        compiler_params=pltpu.CompilerParams(vmem_limit_bytes=60 * 2**20),
        cost_estimate=pl.CostEstimate(flops=10**10, bytes_accessed=2**20, transcendentals=0),
        name="pack_tokens",
    )(tokens, routes_t, weights_t)


def collect(blocks, *earlier):
    nb, h = len(blocks), blocks[0].shape[0]

    def body(*refs):
        for i in range(nb):
            refs[-1][i * h : (i + 1) * h, :] = refs[i][...]

    shape = jax.ShapeDtypeStruct((nb * h, blocks[0].shape[1]), BF)
    return on_chip(body, [*blocks, *earlier], [shape], 0, "collect")[0]


TOKEN = jax.ShapeDtypeStruct((8, 128), F32)


def forward(place, near, far, gate, up, down, T, e_total):
    E, D, F = gate.shape
    step = T + extra_rows(e_total, T, D)
    nb = near.shape[0] // step
    rows, wide, per = 2 * nb * T, E * F, e_total * T // D

    def body(place_ref, near_in, far_in, gate_ref, up_ref, down_ref, *refs):
        hid_refs, wa_refs, wb_refs = refs[0:2], refs[2:4], refs[4:6]
        hwt_ref, tokt_ref, near_ref, far_ref, token_ref, buf = refs[6:]
        token_ref[...] = jnp.zeros_like(token_ref)
        diagonal = lax.broadcasted_iota(jnp.int32, (T, T), 0) == lax.broadcasted_iota(
            jnp.int32, (T, T), 1
        )
        sublane = lax.broadcasted_iota(jnp.int32, (buf.shape[0], T), 0)
        buf[...] = jnp.zeros_like(buf)
        for side, source in enumerate((near_in, far_in)):
            for i in range(0, nb, 2):
                xs, ws = [], [[] for _ in range(E)]
                for b in (i, i + 1):
                    xs.append(source[b * step : b * step + T, :])
                    packed = source[b * step + T : (b + 1) * step, :].astype(F32)
                    buf[:per, :] = (
                        packed[:per] + packed[per : 2 * per] + packed[2 * per : 3 * per]
                    )
                    for j in range(E):
                        flat = (place_ref[2] * E + j) * T
                        at = pl.ds(pl.multiple_of(flat % D, T), T)
                        row = jnp.where(sublane == flat // D, buf[:, at], 0.0)
                        row = jnp.broadcast_to(jnp.sum(row, axis=0, keepdims=True), (T, T))
                        ws[j].append(
                            jnp.sum(jnp.where(diagonal, row, 0.0), axis=1, keepdims=True)
                        )
                x = jnp.concatenate(xs, axis=0)
                here = slice(i * T, (i + 2) * T)
                at = slice((side * nb + i) * T, (side * nb + i + 2) * T)
                tokt_ref[:, at] = x.T
                part = jnp.zeros((2 * T, D), F32)
                for j in range(E):
                    cols = slice(j * F, (j + 1) * F)
                    g = mm(x, gate_ref[j])
                    u = mm(x, up_ref[j])
                    w = jnp.concatenate(ws[j], axis=0)
                    s = jax.nn.sigmoid(g)
                    a = g * s
                    hid = a * u
                    hid_refs[side][here, cols] = hid.astype(BF)
                    wa_refs[side][here, cols] = (w * a).astype(BF)
                    wb_refs[side][here, cols] = (w * (u * s * (1.0 + g * (1.0 - s)))).astype(BF)
                    scaled = (w * hid).astype(BF)
                    hwt_ref[cols, at] = scaled.T
                    part = part + mm(scaled, down_ref[j])
                if side == 0:
                    near_ref[here, :] = part
                else:
                    far_ref[here, :] = part.astype(BF)

    out_shape = [jax.ShapeDtypeStruct((rows // 2, wide), BF)] * 6 + [
        jax.ShapeDtypeStruct((wide, rows), BF),
        jax.ShapeDtypeStruct((D, rows), BF),
        jax.ShapeDtypeStruct((rows // 2, D), F32),
        jax.ShapeDtypeStruct((rows // 2, D), BF),
        TOKEN,
    ]
    return on_chip(
        body,
        [place, near, far, gate, up, down],
        out_shape,
        6 * rows * D * wide,
        "forward",
        scalars=1,
        scratch=[pltpu.VMEM((-(-per // 8) * 8, D), F32)],
    )


def hidden_grads(cot, hid, wa, wb, down, *earlier):
    E, F, D = down.shape
    rows, wide = cot.shape[0], E * F
    step = 256

    def body(*refs):
        cot_ref, hid_ref, wa_ref, wb_ref, down_ref = refs[:5]
        gg_ref, ug_ref, rg_ref, token_ref = refs[5 + len(earlier) :]
        token_ref[...] = jnp.zeros_like(token_ref)
        lane = lax.broadcasted_iota(jnp.int32, (step, 128), 1)
        for m in range(0, rows, step):
            at = slice(m, m + step)
            c = cot_ref[at, :]
            total = jnp.zeros((step, 128), F32)
            for j in range(E):
                cols = slice(j * F, (j + 1) * F)
                h = mm_nt(c, down_ref[j])
                gg_ref[at, cols] = (h * wb_ref[at, cols].astype(F32)).astype(BF)
                ug_ref[at, cols] = (h * wa_ref[at, cols].astype(F32)).astype(BF)
                r = jnp.sum(h * hid_ref[at, cols].astype(F32), axis=1, keepdims=True)
                total = jnp.where(lane == j, r, total)
            rg_ref[at, :] = total

    out_shape = [jax.ShapeDtypeStruct((rows, wide), BF)] * 2 + [
        jax.ShapeDtypeStruct((rows, 128), F32),
        TOKEN,
    ]
    return on_chip(
        body,
        [cot, hid, wa, wb, down, *earlier],
        out_shape,
        2 * rows * D * wide,
        "hidden_grads",
    )


def token_partials(place, gg, ug, rg, gate, up, T, e_total, *earlier):
    half, wide = gg[0].shape
    E, D, F = gate.shape
    extra = extra_rows(e_total, T, D)
    step, nb, per = T + extra, half // T, e_total * T // D

    def body(*refs):
        place_ref = refs[0]
        gg_refs, ug_refs, rg_refs = refs[1:3], refs[3:5], refs[5:7]
        gate_ref, up_ref = refs[7:9]
        near_ref, far_ref, buf = refs[9 + len(earlier) :]
        sublane = lax.broadcasted_iota(jnp.int32, (extra, T), 0)
        for side in range(2):
            for i in range(0, nb, 2):
                at = slice(i * T, (i + 2) * T)
                part = jnp.zeros((2 * T, D), F32)
                for j in range(E):
                    cols = slice(j * F, (j + 1) * F)
                    part = part + mm_nt(gg_refs[side][at, cols], gate_ref[j])
                    part = part + mm_nt(ug_refs[side][at, cols], up_ref[j])
                for b in (i, i + 1):
                    buf[...] = jnp.zeros_like(buf)
                    turned = rg_refs[side][b * T : (b + 1) * T, :].T
                    for p, third in enumerate(thirds(turned[:8, :])):
                        for j in range(E):
                            flat = (place_ref[2] * E + j) * T
                            lanes = pl.ds(pl.multiple_of(flat % D, T), T)
                            mine = jnp.broadcast_to(third[j : j + 1, :], (extra, T))
                            row = sublane == p * per + flat // D
                            buf[:, lanes] = jnp.where(row, mine, buf[:, lanes])
                    mine = part[(b - i) * T : (b - i + 1) * T]
                    if side == 0:
                        near_ref[b * step : b * step + T, :] = mine
                        near_ref[b * step + T : (b + 1) * step, :] = buf[...]
                    else:
                        far_ref[b * step : b * step + T, :] = mine.astype(BF)
                        far_ref[b * step + T : (b + 1) * step, :] = buf[...].astype(BF)

    out_shape = [
        jax.ShapeDtypeStruct((nb * step, D), F32),
        jax.ShapeDtypeStruct((nb * step, D), BF),
    ]
    return on_chip(
        body,
        [place, *gg, *ug, *rg, gate, up, *earlier],
        out_shape,
        8 * half * D * wide,
        "token_partials",
        scalars=1,
        scratch=[pltpu.VMEM((extra, D), F32)],
    )


def weight_partials(place, lhs_t, rhs, experts, n, out_rows, name, *earlier):
    r = out_rows // (n * n)
    rows = lhs_t.shape[1]
    half = rows // 2
    joined = lhs_t.shape[0] != out_rows
    width = rhs[0].shape[1] // (1 if joined else experts)
    per = n * n if joined else 0

    def body(place_ref, left_ref, *refs):
        xi, yi = place_ref[0], place_ref[1]
        outs = refs[2 + len(earlier) : -1]
        refs[-1][...] = jnp.zeros_like(refs[-1])
        for k in [*range(1, n), 0]:
            for j in range(experts):
                left = []
                for q in range(n):
                    a, b = (k, q) if j % 2 == 0 else (q, k)
                    block = j * per + ((yi + b) % n) * n + (xi + a) % n
                    left.append(left_ref[pl.ds(pl.multiple_of(block * r, r), r), :])
                left = jnp.concatenate(left, axis=0)
                cols = slice(0, width) if joined else slice(j * width, (j + 1) * width)
                part = mm(left[:, :half], refs[0][:, cols]) + mm(left[:, half:], refs[1][:, cols])
                part = part.reshape(n, r, width)
                if k:
                    outs[2 * j][k - 1] = part.astype(BF)
                else:
                    outs[2 * j + 1][...] = part

    out_shape = [
        jax.ShapeDtypeStruct((n - 1, n, r, width), BF),
        jax.ShapeDtypeStruct((n, r, width), F32),
    ] * experts + [TOKEN]
    outs = on_chip(
        body,
        [place, lhs_t, *rhs, *earlier],
        out_shape,
        2 * experts * out_rows * width * rows,
        name,
        scalars=1,
    )
    return [(outs[2 * j], outs[2 * j + 1]) for j in range(experts)], outs[-1]


def add_first(parts, got, n, name, *earlier):
    E = len(parts)
    _, r, width = parts[0][1].shape

    def body(*refs):
        ins, outs = refs[: E * n], refs[E * n + len(earlier) :]
        outs[-1][...] = jnp.zeros_like(outs[-1])
        for j in range(E):
            for q in range(n):
                total = ins[j * n][q]
                for k in range(1, n):
                    total = total + ins[j * n + k][q].astype(F32)
                out = outs[j * n + q]
                out[...] = total.astype(out.dtype)

    operands = [v for j in range(E) for v in (parts[j][1], *got[j])]
    shapes = [jax.ShapeDtypeStruct((r, width), F32 if q == 0 else BF) for q in range(n)] * E
    outs = on_chip(body, [*operands, *earlier], shapes + [TOKEN], 0, name)
    return [outs[j * n : (j + 1) * n] for j in range(E)], outs[-1]


def collect_relayed(place, own, two, up, down, relayed, *earlier):
    h = own.shape[0]

    def body(place_ref, own_ref, two_ref, up_ref, down_ref, relayed_ref, *refs):
        out_ref = refs[-1]
        z = place_ref[2] // 2
        out_ref[:h, :] = own_ref[...]
        out_ref[2 * h : 3 * h, :] = two_ref[...]

        @pl.when(z == 0)
        def _():
            out_ref[h : 2 * h, :] = relayed_ref[...]

        @pl.when(z != 0)
        def _():
            out_ref[h : 2 * h, :] = up_ref[...]

        @pl.when(z == 3)
        def _():
            out_ref[3 * h :, :] = relayed_ref[...]

        @pl.when(z != 3)
        def _():
            out_ref[3 * h :, :] = down_ref[...]

    shape = jax.ShapeDtypeStruct((4 * h, own.shape[1]), BF)
    operands = [place, own, two, up, down, relayed, *earlier]
    return on_chip(body, operands, [shape], 0, "collect", scalars=1)[0]


def relay(totals, name, *earlier):
    sent = [v for total in totals for v in total[1:]]

    def body(*refs):
        outs = refs[len(sent) + len(earlier) :]
        outs[-1][...] = jnp.zeros_like(outs[-1])
        for source, out in zip(refs, outs[:-1]):
            out[...] = source[...]

    shapes = [jax.ShapeDtypeStruct(v.shape, v.dtype) for v in sent]
    *outs, done = on_chip(body, [*sent, *earlier], shapes + [TOKEN], 0, name)
    per = len(sent) // len(totals)
    return [[t[0], *outs[i * per : (i + 1) * per]] for i, t in enumerate(totals)], done


def add_second(totals, got, n, name, *earlier):
    E = len(totals)
    r, width = totals[0][0].shape

    def body(*refs):
        ins, (out_ref, token_ref) = refs[: E * n], refs[E * n + len(earlier) :]
        token_ref[...] = jnp.zeros_like(token_ref)
        for j in range(E):
            total = ins[j * n][...]
            for k in range(1, n):
                total = total + ins[j * n + k][...].astype(F32)
            out_ref[j] = total

    operands = [v for j in range(E) for v in (totals[j][0], *got[j])]
    return on_chip(
        body,
        [*operands, *earlier],
        [jax.ShapeDtypeStruct((E, r, width), F32), TOKEN],
        0,
        name,
    )


def add_sides(place, near, far, nz, name, *earlier):
    step, D = near.shape[0] // nz, near.shape[1]

    def body(place_ref, near_ref, far_ref, *refs):
        out_ref, token_ref = refs[len(earlier) :]
        token_ref[...] = jnp.zeros_like(token_ref)
        z = place_ref[2] // 2
        for k in range(nz):
            at = slice(k * step, (k + 1) * step)
            total = near_ref[at, :] + far_ref[at, :].astype(F32)
            to = pl.multiple_of((z - k + nz) % nz * step, step)
            out_ref[pl.ds(to, step), :] = total.astype(BF)

    shapes = [jax.ShapeDtypeStruct((nz * step, D), BF), TOKEN]
    return on_chip(body, [place, near, far, *earlier], shapes, 0, name, scalars=1)


def split_sides(near, far, nz, name, *earlier):
    step, D = near.shape[0] // nz, near.shape[1]

    def body(near_ref, far_ref, *refs):
        outs = refs[len(earlier) :]
        for k in range(nz):
            at = slice(k * step, (k + 1) * step)
            total = near_ref[at, :] + far_ref[at, :].astype(F32)
            outs[k][...] = total.astype(outs[k].dtype)

    shapes = [jax.ShapeDtypeStruct((step, D), F32 if k == 0 else BF) for k in range(nz)]
    return on_chip(body, [near, far, *earlier], shapes, 0, name)


def sum_rows(own, got, name, *earlier):
    def body(*refs):
        total = refs[0][...]
        for g in refs[1 : 1 + len(got)]:
            total = total + g[...].astype(F32)
        refs[-2][...] = total.astype(BF)
        refs[-1][...] = jnp.zeros_like(refs[-1])

    shapes = [jax.ShapeDtypeStruct(own.shape, BF), TOKEN]
    return on_chip(body, [own, *got, *earlier], shapes, 0, name)


def sum_rows_and_routes(got, routes_t, nz, e_total, name):
    top, T = routes_t.shape
    step, D = got.shape[0] // nz, got.shape[1]
    per, lanes = e_total * T // D, D // T

    def body(*refs):
        routes_ref, got_ref, rows_ref, routes_out, token_ref = refs
        token_ref[...] = jnp.zeros_like(token_ref)
        total = got_ref[:step, :].astype(F32)
        for k in range(1, nz):
            total = total + got_ref[k * step : (k + 1) * step, :].astype(F32)
        rows_ref[...] = total[:T].astype(BF)
        packed = total[T:]
        packed = packed[:per] + packed[per : 2 * per] + packed[2 * per : 3 * per]
        grads = jnp.zeros((top, T), F32)
        for i in range(e_total):
            at = slice(i % lanes * T, (i % lanes + 1) * T)
            row = packed[i // lanes : i // lanes + 1, at]
            grads = jnp.where(routes_ref[...] == i, row, grads)
        routes_out[...] = grads

    shapes = [
        jax.ShapeDtypeStruct((T, D), BF),
        jax.ShapeDtypeStruct((top, T), F32),
        TOKEN,
    ]
    return on_chip(body, [routes_t, got], shapes, 0, name)


def local(tokens, routes, route_weights, gate_weight, up_weight, down_weight, cotangent):
    dp = lax.axis_size("dp")
    ne = lax.axis_size("expert")
    n = math.isqrt(dp)
    nz = ne // 2
    T, D = tokens.shape
    E, _, F = gate_weight.shape
    e_total = E * ne
    d = lax.axis_index("dp")
    e = lax.axis_index("expert")
    place = jnp.stack([d % n, d // n, e]).astype(jnp.int32)

    def swap(v):
        return lax.ppermute(v, "expert", [(i, i ^ 1) for i in range(ne)])

    def move_z(v, k):
        pairs = [(2 * z + c, 2 * ((z + k) % nz) + c) for z in range(nz) for c in range(2)]
        return lax.ppermute(v, "expert", pairs)

    def move_x(v, k):
        pairs = [(y * n + x, y * n + (x + k) % n) for y in range(n) for x in range(n)]
        return lax.ppermute(v, "dp", pairs)

    def move_y(v, k):
        pairs = [(y * n + x, ((y + k) % n) * n + x) for y in range(n) for x in range(n)]
        return lax.ppermute(v, "dp", pairs)

    def gather_near(v):
        return [v] + [move_z(v, k) for k in range(1, nz)]

    def chip_pairs(pairs):
        return [(2 * a + c, 2 * b + c) for a, b in pairs for c in range(2)]

    def near_rows(v, *earlier):
        if nz != 4:
            return collect(gather_near(v), *earlier)
        send = lambda u, pairs: lax.ppermute(u, "expert", chip_pairs(pairs))
        two = move_z(v, 2)
        up = send(v, [(0, 1), (1, 2), (2, 3)])
        down = send(v, [(1, 0), (2, 1), (3, 2)])
        relayed = send(two, [(2, 3), (1, 0)])
        return collect_relayed(place, v, two, up, down, relayed, *earlier)

    packed = pack_tokens(tokens, routes.T, route_weights.T, e_total)
    token_near = near_rows(packed)
    cot_blocks = gather_near(cotangent)
    token_far = swap(token_near)
    *saved, hw_t, tok_t, out_near, out_far, forward_done = forward(
        place, token_near, token_far, gate_weight, up_weight, down_weight, T, e_total
    )
    hid, wa, wb = saved[0:2], saved[2:4], saved[4:6]
    out_far = swap(out_far)
    cot_near = collect(cot_blocks, forward_done)
    cot_far = swap(cot_near)

    def send_first(parts):
        got = []
        for j, (sent, _) in enumerate(parts):
            move = move_x if j % 2 == 0 else move_y
            got.append([move(sent[k - 1], k) for k in range(1, n)])
        return got

    def send_second(totals):
        got = []
        for j, total in enumerate(totals):
            move = move_y if j % 2 == 0 else move_x
            got.append([move(total[k], k) for k in range(1, n)])
        return got

    z_groups = [[2 * z + c for z in range(nz)] for c in range(2)]

    def send_home(parts):
        return lax.all_to_all(
            parts,
            "expert",
            split_axis=0,
            concat_axis=0,
            tiled=True,
            axis_index_groups=z_groups,
        )

    gg0, ug0, rg0, near_done = hidden_grads(cot_near, hid[0], wa[0], wb[0], down_weight)
    down_part, down_done = weight_partials(
        place, hw_t, [cot_near, cot_far], E, n, F, "down_partials", near_done
    )
    down_got = send_first(down_part)
    gg1, ug1, rg1, _ = hidden_grads(cot_far, hid[1], wa[1], wb[1], down_weight, down_done)
    gate_part, gate_done = weight_partials(place, tok_t, [gg0, gg1], E, n, D, "gate_partials")
    gate_got = send_first(gate_part)
    out_parts = split_sides(out_near, out_far, nz, "out_sides", down_done)
    out_got = [move_z(out_parts[k], -k) for k in range(1, nz)]
    down_totals, down_mid = add_first(down_part, down_got, n, "down_first", gate_done, out_got[0])
    tg_near, tg_far = token_partials(
        place,
        [gg0, gg1],
        [ug0, ug1],
        [rg0, rg1],
        gate_weight,
        up_weight,
        T,
        e_total,
        down_mid,
    )
    tg_far = swap(tg_far)
    up_part, up_done = weight_partials(
        place, tok_t, [ug0, ug1], E, n, D, "up_partials", tg_near[:8, :128]
    )
    up_got = send_first(up_part)
    layer_out, out_done = sum_rows(out_parts[0], out_got, "out_rows", up_done)
    tg_parts, tg_done = add_sides(place, tg_near, tg_far, nz, "token_sides", out_done)
    tg_got = send_home(tg_parts)
    down_totals, down_mid = relay(down_totals, "down_relay", tg_done)
    down_got = send_second(down_totals)
    gate_totals, gate_mid = add_first(gate_part, gate_got, n, "gate_first", down_mid)
    gate_got = send_second(gate_totals)
    up_totals, up_mid = add_first(up_part, up_got, n, "up_first", gate_mid)
    up_got = send_second(up_totals)
    down_grads, down_done = add_second(down_totals, down_got, n, "down_second", up_mid)
    gate_grads, gate_done = add_second(gate_totals, gate_got, n, "gate_second", down_done)
    token_grads, route_grads_t, rows_done = sum_rows_and_routes(
        tg_got, routes.T, nz, e_total, "token_rows"
    )
    up_grads, _ = add_second(up_totals, up_got, n, "up_second", gate_done)
    route_grads = route_grads_t.T

    return (layer_out, token_grads, route_grads, gate_grads, up_grads, down_grads)


def solution(mesh):
    rows = P(("dp", "expert"), None)
    weight = P("expert", None, None)
    grad = P("expert", "dp", None)
    return jax.shard_map(
        local,
        mesh=mesh,
        in_specs=(rows, rows, rows, weight, weight, weight, rows),
        out_specs=(rows, rows, rows, grad, grad, grad),
        check_vma=False,
    )
```
